256 devices in a mesh: pair: 32 (over z, x), virt: 8 (over y, core).
Axes of the slice: x: 4, y: 4, z: 8, core: 2. Of those that a mesh axis runs over, the one named last changes fastest.
Arguments:
- amplitudes: float32 [16, 256, 128, 128], P('virt', 'pair'), may hold values from -6 to 6
- factors: float32 [6, 16, 128, 128], replicated, may hold values from -0.5 to 0.5
- integral_quadruple_table: int32 [6, 16, 16, 3], replicated, may hold values from 0 to 15
- pair_region: int32 [128], replicated, may hold values from 0 to 5
- owner_map: int32 [256], replicated, may hold values from 0 to 31, as said below
Outputs:
- residual: float32 [16, 512, 128, 128], P('virt', 'pair')
The draws below stay inside these ranges and needn't reach their ends.
Inputs may be any that keep to these rules, and one draw needn't show every extreme that they name: `owner_map`: home h holds pairs 8 * h to 8 * h + 7. No two pairs of one home share an owner, so every home sends exactly 1 pair to each owner it uses; no owner has more than 16 pairs, and some owners have exactly 16.
All inputs are finite; a program needn't handle non-finite values.
Results may differ from the reference program's by a relative error of at most 0.0003.
Values sent between devices are 32-bit elements; how exact they have to be, the bound alone decides.
No kernel may reach another device: no remote copies, remote signals or barrier semaphores. Data moves between devices by JAX's collectives and lax.ppermute only.
A program may use at most 128 MiB of HBM per device.

```python
import jax
import jax.numpy as jnp
import numpy as np
from jax import lax

TILE_VIRTUALS = 128
DOM = 4
QUADRUPLE_COUNT = 16
PAIRS_DEV = 8
REGION_COUNT = 6
PAIR_TILE_SLOTS = 16
NF = 16
OCCUPIED_PAIRS = 256
NHALF = 128
OWN_MOST = 16
SEND_MOST = 1
OSLOTS = 512


def draw_owner_map(key, part):
    homes = OCCUPIED_PAIRS // PAIRS_DEV
    key_sigma, key_tau, key_order = jax.random.split(key, 3)
    sigma = jax.random.permutation(key_sigma, homes)
    first_value = sigma[0]
    sigma = jnp.where(sigma == first_value, homes - 1, jnp.where(sigma == homes - 1, first_value, sigma))
    second_value = sigma[2]
    sigma = jnp.where(sigma == second_value, 0, jnp.where(sigma == 0, second_value, sigma))
    tau = jax.random.permutation(key_tau, homes)
    order_keys = jax.random.split(key_order, homes)
    orders = jax.vmap(lambda item: jax.random.permutation(item, PAIRS_DEV))(order_keys)
    group = orders // SEND_MOST
    parity = tau % 2
    spots = (tau - parity)[:, None] + 2 * group
    owner = sigma[spots % homes]
    return owner.reshape(-1).astype(jnp.int32)


def place_ends(drawn, stream_key, smallest, high):
    longest = drawn.shape.index(max(drawn.shape))
    spots = []
    for shift in (0, 1):
        where = [jax.random.randint(jax.random.fold_in(stream_key, axis), (), 0, length) for axis, length in enumerate(drawn.shape)]
        where[longest] = (where[longest] + shift) % drawn.shape[longest]
        spots.append(tuple(where))
    return drawn.at[spots[0]].set(smallest).at[spots[1]].set(high)


def block_levels(rng, extent, shards, least, largest):
    factor_of, own = 1.0, jax.random.fold_in(rng, 6)
    for axis_at, parts in shards:
        steps = jnp.exp(jax.random.uniform(jax.random.fold_in(own, axis_at), (parts,), jnp.float32, least / len(shards), largest / len(shards)))
        factor_of = factor_of * jnp.repeat(steps, extent[axis_at] // parts).reshape([-1 if axis == axis_at else 1 for axis in range(len(extent))])
    return factor_of


def gaussian(rng, extent, spread, reach, pieces=(), kind=jnp.bfloat16):
    values = jax.random.normal(rng, extent, jnp.float32) * spread
    if len(pieces) > 0:
        values = block_levels(rng, extent, pieces, -0.22, 0.18) * values
    return jnp.clip(values, min=-reach, max=reach).astype(kind)


def setup_inputs(seed: int = 0) -> dict:
    key_of = jax.random.split(jax.random.key(seed), 6)
    return {
        "amplitudes": gaussian(key_of[0], (PAIR_TILE_SLOTS, OCCUPIED_PAIRS, TILE_VIRTUALS, TILE_VIRTUALS), 1.0, 6.0, ((0, 8), (1, 32)), jnp.float32),
        "factors": gaussian(key_of[1], (REGION_COUNT, NF, TILE_VIRTUALS, TILE_VIRTUALS), TILE_VIRTUALS ** -0.5, 0.5, (), jnp.float32),
        "integral_quadruple_table": place_ends(jax.random.randint(key_of[2], (REGION_COUNT, PAIR_TILE_SLOTS, QUADRUPLE_COUNT, 3), 0, PAIR_TILE_SLOTS), jax.random.fold_in(key_of[2], 1), 0, PAIR_TILE_SLOTS - 1).astype(jnp.int32),
        "pair_region": place_ends(jax.random.randint(key_of[3], (NHALF,), 0, REGION_COUNT), jax.random.fold_in(key_of[3], 1), 0, REGION_COUNT - 1).astype(jnp.int32),
        "owner_map": draw_owner_map(jax.random.fold_in(key_of[5], 71), 0),
    }


def slot_partner(dom):
    off_diag = dom * (dom - 1)
    return np.array([(slot ^ 1) if slot < off_diag else slot for slot in range(dom * dom)], dtype=np.int32)


def reference(amplitudes, factors, integral_quadruple_table, pair_region, owner_map):
    slot_total = DOM * DOM
    pair_total = amplitudes.shape[1]
    region = jnp.concatenate([pair_region, pair_region]).astype(jnp.int32)

    def pair_ladder(packed):
        amp_tiles, reg = packed
        quad_rows = integral_quadruple_table[reg]
        left_tiles = factors[reg][quad_rows[..., 1]]
        right_tiles = factors[reg][quad_rows[..., 2]]
        inner_prod = jnp.einsum('skab,sbc->skac', left_tiles, amp_tiles, precision=lax.Precision.HIGHEST)
        product = jnp.einsum('skac,skdc->skad', inner_prod, right_tiles, precision=lax.Precision.HIGHEST)
        onehot = (quad_rows[..., 0][..., None] == jnp.arange(slot_total)[None, None, :]).astype(jnp.float32)
        return jnp.einsum('sko,skad->oad', onehot, product, precision=lax.Precision.HIGHEST)

    ladder = lax.map(pair_ladder, (jnp.swapaxes(amplitudes, 0, 1), region))
    mirrored = jnp.roll(ladder, pair_total // 2, axis=0)
    partner = slot_partner(DOM)
    symmetric = ladder + jnp.swapaxes(mirrored[:, partner], -1, -2)
    owners = OSLOTS // OWN_MOST
    owned_mask = owner_map[None, :] == jnp.arange(owners, dtype=jnp.int32)[:, None]
    owner_rank = jnp.cumsum(owned_mask.astype(jnp.int32), axis=1) - 1
    rank_of_pair = jnp.sum(jnp.where(owned_mask, owner_rank, 0), axis=0).astype(jnp.int32)
    out_slot = (owner_map * OWN_MOST + rank_of_pair).astype(jnp.int32)
    result = jnp.zeros((owners * OWN_MOST, slot_total, TILE_VIRTUALS, TILE_VIRTUALS), jnp.float32).at[out_slot].set(symmetric)
    return jnp.swapaxes(result, 0, 1)
```

```python
import jax
import jax.numpy as jnp
from jax import lax
from jax.experimental import pallas as pl
from jax.experimental.pallas import tpu as pltpu
from jax.sharding import PartitionSpec as P

DOM = 4
OFF_DIAG = DOM * (DOM - 1)
F32 = jnp.float32
BF16 = jnp.bfloat16


def halves(x):
    high = x.astype(BF16)
    return high, (x - high.astype(F32)).astype(BF16)


def ladder_body(
    codes, info, even, odd, fac, out, f_pair, f_turn, amp_high, amp_low, prod, grouped
):
    slots, n, _ = out.shape
    mirrored = info[1]

    def split_factor(l, c):
        tile = fac[0, l]
        rows = pl.ds(pl.multiple_of(l * n, n), n)
        high, low = halves(tile)
        f_pair[rows, :n] = high
        f_pair[rows, n:] = low
        high, low = halves(tile.T)
        f_turn[rows, :n] = high
        f_turn[rows, n:] = low
        return c

    lax.fori_loop(0, slots, split_factor, 0)

    def put_amp(i, v, tile):
        high, low = halves(tile)
        amp_high[v, :, i * n : (i + 1) * n] = high
        amp_low[v, :, i * n : (i + 1) * n] = low

    @pl.when(mirrored == 0)
    def _():
        def go(v, c):
            put_amp(0, v, even[v])
            put_amp(1, v, odd[v])
            return c

        lax.fori_loop(0, slots // 2, go, 0)

    @pl.when(mirrored != 0)
    def _():
        def go(v, c):
            put_amp(0, v, even[v].T)
            put_amp(1, v, odd[v].T)
            return c

        lax.fori_loop(0, slots // 2, go, 0)

    def clear(r, c):
        grouped[r] = jnp.zeros(grouped.shape[1:], F32)
        return c

    lax.fori_loop(0, slots, clear, 0)

    def one_amp_pair(v, c):
        high = amp_high[v]
        prod[...] = jnp.dot(
            f_pair[...], jnp.concatenate([high, high], axis=0), preferred_element_type=F32
        ) + jnp.dot(f_pair[:, :n], amp_low[v], preferred_element_type=F32)
        for i in range(2):

            def entry(k, c):
                code = codes[2 * v + i, k]
                o = code // 256
                l = (code // 16) % 16
                r = code % 16
                to = pl.ds(pl.multiple_of(o * n, n), n)
                grouped[r, to, :] += prod[
                    pl.ds(pl.multiple_of(l * n, n), n), i * n : (i + 1) * n
                ]
                return c

            lax.fori_loop(0, codes.shape[1], entry, 0, unroll=4)
        return c

    lax.fori_loop(0, slots // 2, one_amp_pair, 0)

    step = 4

    def one_out(g, c):
        rows = pl.ds(pl.multiple_of(g * (step * n), step * n), step * n)
        parts = [halves(grouped[r, rows, :]) for r in range(slots)]
        high = jnp.concatenate([a for a, _ in parts], axis=1)
        low = jnp.concatenate([b for _, b in parts], axis=1)
        both = jnp.dot(high, f_turn[...], preferred_element_type=F32)
        rest = jnp.dot(low, f_turn[:, :n], preferred_element_type=F32)
        total = both[:, :n] + both[:, n:] + rest
        out[pl.ds(g * step, step)] = total.reshape(step, n, n)
        return c

    lax.fori_loop(0, slots // step, one_out, 0)


def ladder(codes, info, even, odd, factors):
    slots = 2 * even.shape[0]
    n = even.shape[-1]
    whole = pl.BlockSpec((slots // 2, n, n), lambda i, *_: (0, 0, 0))
    wide = slots * n
    return pl.pallas_call(
        ladder_body,
        out_shape=jax.ShapeDtypeStruct((slots, n, n), F32),
        grid_spec=pltpu.PrefetchScalarGridSpec(
            num_scalar_prefetch=2,
            grid=(1,),
            in_specs=[
                whole,
                whole,
                pl.BlockSpec((1, slots, n, n), lambda i, codes, info: (info[0], 0, 0, 0)),
            ],
            out_specs=pl.BlockSpec((slots, n, n), lambda i, *_: (0, 0, 0)),
            scratch_shapes=[
                pltpu.VMEM((wide, 2 * n), BF16),
                pltpu.VMEM((wide, 2 * n), BF16),
                pltpu.VMEM((slots // 2, n, 2 * n), BF16),
                pltpu.VMEM((slots // 2, n, 2 * n), BF16),
                pltpu.VMEM((wide, 2 * n), F32),
                pltpu.VMEM((slots, wide, n), F32),
            ],
        ),
        compiler_params=pltpu.CompilerParams(vmem_limit_bytes=48 << 20),
        cost_estimate=pl.CostEstimate(
            flops=12 * wide * wide * n, bytes_accessed=4 << 20, transcendentals=0
        ),
        name="ladder",
    )(codes, info, even, odd, factors)


def pairs_body(spot, blocks, out, *, per_home):
    count = blocks.shape[0]
    homes = count // per_home
    half = count // 2
    out[...] = jnp.zeros(out.shape, F32)

    def one(q, c):
        row = (q % per_home) * homes + q // per_home
        value = blocks[row] + blocks[row + homes // 2]
        out[spot[q]] = value
        out[spot[q + half]] = value
        return c

    lax.fori_loop(0, half, one, 0, unroll=4)


def join_pairs(spot, blocks, own_slots, per_home):
    def body(spot, blocks, out):
        pairs_body(spot, blocks, out, per_home=per_home)

    return pl.pallas_call(
        body,
        out_shape=jax.ShapeDtypeStruct((own_slots,) + blocks.shape[1:], F32),
        grid_spec=pltpu.PrefetchScalarGridSpec(
            num_scalar_prefetch=1,
            grid=(1,),
            in_specs=[pl.BlockSpec(blocks.shape, lambda i, *_: (0, 0, 0))],
            out_specs=pl.BlockSpec((own_slots,) + blocks.shape[1:], lambda i, *_: (0, 0, 0)),
        ),
        compiler_params=pltpu.CompilerParams(vmem_limit_bytes=16 << 20),
        cost_estimate=pl.CostEstimate(flops=1 << 18, bytes_accessed=3 << 20, transcendentals=0),
        name="join_pairs",
    )(spot, blocks)


def settle(info, blocks, own_most, local_slots, n, group):
    parts = blocks.shape[0]
    per = parts // local_slots

    def body(info, src, out):
        plain = info[0]
        swap = info[1]
        for g in range(group):
            k = pl.program_id(0) * group + g

            @pl.when(k < plain)
            def _():
                for i in range(local_slots):
                    out[i, g] = src[i * per : (i + 1) * per, g].reshape(n, n)

            @pl.when(k >= plain)
            def _():
                for i in range(local_slots):
                    base = jnp.where(swap != 0, local_slots - 1 - i, i) * per
                    out[i, g] = src[pl.ds(base, per), g].reshape(n, n).T

    return pl.pallas_call(
        body,
        out_shape=jax.ShapeDtypeStruct((local_slots, own_most, n, n), F32),
        grid_spec=pltpu.PrefetchScalarGridSpec(
            num_scalar_prefetch=1,
            grid=(own_most // group,),
            in_specs=[
                pl.BlockSpec(
                    (parts, group) + blocks.shape[2:], lambda i, *_: (0, i, 0, 0)
                )
            ],
            out_specs=pl.BlockSpec((local_slots, group, n, n), lambda i, *_: (0, i, 0, 0)),
        ),
        compiler_params=pltpu.CompilerParams(vmem_limit_bytes=16 << 20),
        cost_estimate=pl.CostEstimate(flops=1 << 18, bytes_accessed=4 << 20, transcendentals=0),
        name="settle",
    )(info, blocks)


def on_device(amplitudes, factors, integral_quadruple_table, pair_region, owner_map):
    pair_count = lax.axis_size("pair")
    virt_count = lax.axis_size("virt")
    my_pair = lax.axis_index("pair")
    my_virt = lax.axis_index("virt")
    local_slots, per_home, n, _ = amplitudes.shape
    pair_total = owner_map.shape[0]
    half = pair_total // 2
    own_most = 2 * per_home

    pair = my_pair * per_home + my_virt
    mirrored = (pair >= half).astype(jnp.int32)
    region = pair_region[pair % half]
    rows = integral_quadruple_table[region]
    o, left, right = rows[..., 0], rows[..., 1], rows[..., 2]
    partner = jnp.where(o < OFF_DIAG, o ^ 1, o)
    codes = jnp.where(
        mirrored != 0, partner * 256 + right * 16 + left, o * 256 + left * 16 + right
    )
    info = jnp.stack([region, mirrored])

    same = (owner_map[:, None] == owner_map[None, :]) & (
        jnp.arange(pair_total)[None, :] < jnp.arange(pair_total)[:, None]
    )
    spot = owner_map * own_most + jnp.sum(same.astype(jnp.int32), axis=1)

    even = lax.all_to_all(amplitudes[0], "virt", split_axis=0, concat_axis=0, tiled=True)
    odd = lax.all_to_all(amplitudes[1], "virt", split_axis=0, concat_axis=0, tiled=True)
    result = ladder(codes, info, even, odd, factors)
    sheets = result.reshape(virt_count * pair_count, -1, n)
    spread = lax.all_to_all(sheets, ("virt", "pair"), split_axis=0, concat_axis=0, tiled=True)
    joined = join_pairs(spot, spread, pair_count * own_most, per_home)
    arrived = lax.all_to_all(joined, "pair", split_axis=0, concat_axis=0, tiled=True)
    plain = jnp.sum((owner_map[:half] == my_pair).astype(jnp.int32))
    swap = (my_virt * local_slots < OFF_DIAG).astype(jnp.int32)
    return settle(
        jnp.stack([plain, swap]),
        arrived.reshape(pair_count, own_most, -1, n),
        own_most,
        local_slots,
        n,
        4,
    )


def solution(mesh):
    return jax.shard_map(
        on_device,
        mesh=mesh,
        in_specs=(P("virt", "pair", None, None), P(), P(), P(), P()),
        out_specs=P("virt", "pair", None, None),
        check_vma=False,
    )
```

```python
import jax
import jax.numpy as jnp
from jax import lax
from jax.experimental import pallas as pl
from jax.experimental.pallas import tpu as pltpu
from jax.sharding import PartitionSpec as P

DOM = 4
OFF_DIAG = DOM * (DOM - 1)
F32 = jnp.float32
BF16 = jnp.bfloat16


def halves(x):
    high = x.astype(BF16)
    return high, (x - high.astype(F32)).astype(BF16)


def split_body(info, fac, f_pair, f_turn):
    slots, n = fac.shape[1], fac.shape[2]
    for l in range(slots):
        tile = fac[0, l]
        rows = slice(l * n, (l + 1) * n)
        f_pair[rows, :n], f_pair[rows, n:] = halves(tile)
        f_turn[rows, :n], f_turn[rows, n:] = halves(tile.T)


def split_factors(info, factors):
    _, slots, n, _ = factors.shape
    shape = jax.ShapeDtypeStruct((slots * n, 2 * n), BF16)
    spec = pl.BlockSpec(shape.shape, lambda i, *_: (0, 0))
    return pl.pallas_call(
        split_body,
        out_shape=[shape, shape],
        grid_spec=pltpu.PrefetchScalarGridSpec(
            num_scalar_prefetch=1,
            grid=(1,),
            in_specs=[pl.BlockSpec((1, slots, n, n), lambda i, info: (info[0], 0, 0, 0))],
            out_specs=[spec, spec],
        ),
        compiler_params=pltpu.CompilerParams(vmem_limit_bytes=16 << 20),
        cost_estimate=pl.CostEstimate(flops=1 << 20, bytes_accessed=3 << 20, transcendentals=0),
        name="split_factors",
    )(info, factors)


def ladder_body(codes, info, amp, f_pair, f_turn, out, amp_high, amp_low, prod, grouped):
    slots, n, _ = out.shape
    mirrored = info[1]

    def put(s, tile):
        v, i = s // 2, s % 2
        high, low = halves(tile)
        amp_high[v, :n, i * n : (i + 1) * n] = high
        amp_high[v, n:, i * n : (i + 1) * n] = high
        amp_low[v, :, i * n : (i + 1) * n] = low

    @pl.when(mirrored == 0)
    def _():
        for s in range(slots):
            put(s, amp[s])

    @pl.when(mirrored != 0)
    def _():
        for s in range(slots):
            put(s, amp[s].T)

    def clear(r, c):
        grouped[r] = jnp.zeros(grouped.shape[1:], F32)
        return c

    lax.fori_loop(0, slots, clear, 0)

    def one_amp_pair(v, c):
        prod[...] = jnp.dot(
            f_pair[...], amp_high[v], preferred_element_type=F32
        ) + jnp.dot(f_pair[:, :n], amp_low[v], preferred_element_type=F32)
        for i in range(2):
            for k in range(codes.shape[1]):
                code = codes[2 * v + i, k]
                to = pl.ds(pl.multiple_of((code >> 8) * n, n), n)
                source = pl.ds(pl.multiple_of(((code >> 4) & 15) * n, n), n)
                grouped[code & 15, to, :] += prod[source, i * n : (i + 1) * n]
        return c

    lax.fori_loop(0, slots // 2, one_amp_pair, 0)

    step = 8

    def some_out(g, c):
        rows = pl.ds(pl.multiple_of(g * (step * n), step * n), step * n)
        parts = [halves(grouped[r, rows, :]) for r in range(slots)]
        high = jnp.concatenate([a for a, _ in parts], axis=1)
        low = jnp.concatenate([b for _, b in parts], axis=1)
        both = jnp.dot(high, f_turn[...], preferred_element_type=F32)
        rest = jnp.dot(low, f_turn[:, :n], preferred_element_type=F32)
        total = both[:, :n] + both[:, n:] + rest
        out[pl.ds(g * step, step)] = total.reshape(step, n, n)
        return c

    lax.fori_loop(0, slots // step, some_out, 0)


def ladder(codes, info, amp, f_pair, f_turn):
    slots, n, _ = amp.shape
    wide = slots * n
    whole = pl.BlockSpec((slots, n, n), lambda i, *_: (0, 0, 0))
    table = pl.BlockSpec((wide, 2 * n), lambda i, *_: (0, 0))
    return pl.pallas_call(
        ladder_body,
        out_shape=jax.ShapeDtypeStruct((slots, n, n), F32),
        grid_spec=pltpu.PrefetchScalarGridSpec(
            num_scalar_prefetch=2,
            grid=(1,),
            in_specs=[whole, table, table],
            out_specs=whole,
            scratch_shapes=[
                pltpu.VMEM((slots // 2, 2 * n, 2 * n), BF16),
                pltpu.VMEM((slots // 2, n, 2 * n), BF16),
                pltpu.VMEM((wide, 2 * n), F32),
                pltpu.VMEM((slots, wide, n), F32),
            ],
        ),
        compiler_params=pltpu.CompilerParams(vmem_limit_bytes=48 << 20),
        cost_estimate=pl.CostEstimate(
            flops=12 * wide * wide * n, bytes_accessed=4 << 20, transcendentals=0
        ),
        name="ladder",
    )(codes, info, amp, f_pair, f_turn)


def pairs_body(spot, blocks, out, *, per_home):
    count = blocks.shape[0]
    homes = count // per_home
    half = count // 2
    out[...] = jnp.zeros(out.shape, F32)

    def one(q, c):
        row = (q % per_home) * homes + q // per_home
        value = blocks[row] + blocks[row + homes // 2]
        out[spot[q]] = value
        out[spot[q + half]] = value
        return c

    lax.fori_loop(0, half, one, 0, unroll=4)


def join_pairs(spot, blocks, own_slots, per_home):
    def body(spot, blocks, out):
        pairs_body(spot, blocks, out, per_home=per_home)

    return pl.pallas_call(
        body,
        out_shape=jax.ShapeDtypeStruct((own_slots,) + blocks.shape[1:], F32),
        grid_spec=pltpu.PrefetchScalarGridSpec(
            num_scalar_prefetch=1,
            grid=(1,),
            in_specs=[pl.BlockSpec(blocks.shape, lambda i, *_: (0, 0, 0))],
            out_specs=pl.BlockSpec((own_slots,) + blocks.shape[1:], lambda i, *_: (0, 0, 0)),
        ),
        compiler_params=pltpu.CompilerParams(vmem_limit_bytes=56 << 20),
        cost_estimate=pl.CostEstimate(flops=1 << 18, bytes_accessed=3 << 20, transcendentals=0),
        name="join_pairs",
    )(spot, blocks)


def settle(info, blocks, own_most, local_slots, n, group):
    parts = blocks.shape[0]
    per = parts // local_slots

    def body(info, src, out):
        plain = info[0]
        swap = info[1]
        for g in range(group):
            k = pl.program_id(0) * group + g

            @pl.when(k < plain)
            def _():
                for i in range(local_slots):
                    out[i, g] = src[i * per : (i + 1) * per, g].reshape(n, n)

            @pl.when(k >= plain)
            def _():
                for i in range(local_slots):
                    base = jnp.where(swap != 0, local_slots - 1 - i, i) * per
                    out[i, g] = src[pl.ds(base, per), g].reshape(n, n).T

    return pl.pallas_call(
        body,
        out_shape=jax.ShapeDtypeStruct((local_slots, own_most, n, n), F32),
        grid_spec=pltpu.PrefetchScalarGridSpec(
            num_scalar_prefetch=1,
            grid=(own_most // group,),
            in_specs=[
                pl.BlockSpec(
                    (parts, group) + blocks.shape[2:], lambda i, *_: (0, i, 0, 0)
                )
            ],
            out_specs=pl.BlockSpec((local_slots, group, n, n), lambda i, *_: (0, i, 0, 0)),
        ),
        compiler_params=pltpu.CompilerParams(vmem_limit_bytes=16 << 20),
        cost_estimate=pl.CostEstimate(flops=1 << 18, bytes_accessed=4 << 20, transcendentals=0),
        name="settle",
    )(info, blocks)


def on_device(amplitudes, factors, integral_quadruple_table, pair_region, owner_map):
    pair_count = lax.axis_size("pair")
    virt_count = lax.axis_size("virt")
    my_pair = lax.axis_index("pair")
    my_virt = lax.axis_index("virt")
    local_slots, per_home, n, _ = amplitudes.shape
    pair_total = owner_map.shape[0]
    half = pair_total // 2
    own_most = 2 * per_home

    pair = my_pair * per_home + my_virt
    mirrored = (pair >= half).astype(jnp.int32)
    region = pair_region[pair % half]
    rows = integral_quadruple_table[region]
    o, left, right = rows[..., 0], rows[..., 1], rows[..., 2]
    partner = jnp.where(o < OFF_DIAG, o ^ 1, o)
    codes = jnp.where(
        mirrored != 0, partner * 256 + right * 16 + left, o * 256 + left * 16 + right
    )
    info = jnp.stack([region, mirrored])

    same = (owner_map[:, None] == owner_map[None, :]) & (
        jnp.arange(pair_total)[None, :] < jnp.arange(pair_total)[:, None]
    )
    spot = owner_map * own_most + jnp.sum(same.astype(jnp.int32), axis=1)

    plain = jnp.sum((owner_map[:half] == my_pair).astype(jnp.int32))
    swap = (my_virt * local_slots < OFF_DIAG).astype(jnp.int32)
    settle_info = jnp.stack([plain, swap])

    amp = lax.all_to_all(amplitudes, "virt", split_axis=1, concat_axis=0, tiled=True)
    f_pair, f_turn = split_factors(info, factors)
    amp, codes, info, f_pair, f_turn, spot, settle_info = lax.optimization_barrier(
        (amp, codes, info, f_pair, f_turn, spot, settle_info)
    )
    result = ladder(codes, info, amp.reshape(-1, n, n), f_pair, f_turn)
    sheets = result.reshape(virt_count * pair_count, -1, n)
    spread = lax.all_to_all(sheets, ("virt", "pair"), split_axis=0, concat_axis=0, tiled=True)
    joined = join_pairs(spot, spread, pair_count * own_most, per_home)
    arrived = lax.all_to_all(joined, "pair", split_axis=0, concat_axis=0, tiled=True)
    return settle(
        settle_info,
        arrived.reshape(pair_count, own_most, -1, n),
        own_most,
        local_slots,
        n,
        4,
    )


def solution(mesh):
    return jax.shard_map(
        on_device,
        mesh=mesh,
        in_specs=(P("virt", "pair", None, None), P(), P(), P(), P()),
        out_specs=P("virt", "pair", None, None),
        check_vma=False,
    )
```

```python
import functools

import jax
import jax.numpy as jnp
from jax import lax
from jax.experimental import pallas as pl
from jax.experimental.pallas import tpu as pltpu
from jax.sharding import PartitionSpec as P

DOM = 4
OFF_DIAG = DOM * (DOM - 1)
F32 = jnp.float32
BF16 = jnp.bfloat16
FIRST = 1 << 12


def halves(x):
    high = x.astype(BF16)
    return high, (x - high.astype(F32)).astype(BF16)


def split_body(info, fac, f_pair, f_turn):
    slots, n = fac.shape[1], fac.shape[2]
    for l in range(slots):
        tile = fac[0, l]
        rows = slice(l * n, (l + 1) * n)
        f_pair[rows, :n], f_pair[rows, n:] = halves(tile)
        f_turn[rows, :n], f_turn[rows, n:] = halves(tile.T)


def split_factors(info, factors):
    _, slots, n, _ = factors.shape
    shape = jax.ShapeDtypeStruct((slots * n, 2 * n), BF16)
    spec = pl.BlockSpec(shape.shape, lambda i, *_: (0, 0))
    return pl.pallas_call(
        split_body,
        out_shape=[shape, shape],
        grid_spec=pltpu.PrefetchScalarGridSpec(
            num_scalar_prefetch=1,
            grid=(1,),
            in_specs=[pl.BlockSpec((1, slots, n, n), lambda i, info: (info[0], 0, 0, 0))],
            out_specs=[spec, spec],
        ),
        compiler_params=pltpu.CompilerParams(vmem_limit_bytes=16 << 20),
        cost_estimate=pl.CostEstimate(flops=1 << 20, bytes_accessed=3 << 20, transcendentals=0),
        name="split_factors",
    )(info, factors)


def ladder_body(
    codes, touched, info, amp, f_pair, f_turn, out, amp_high, amp_low, prod_a, prod_b, grouped
):
    slots, n, _ = out.shape
    entries = codes.shape[1]
    mirrored = info[1]

    def put(s, tile):
        v, i = s // 2, s % 2
        high, low = halves(tile)
        amp_high[v, :n, i * n : (i + 1) * n] = high
        amp_high[v, n:, i * n : (i + 1) * n] = high
        amp_low[v, :, i * n : (i + 1) * n] = low

    @pl.when(mirrored == 0)
    def _():
        for s in range(slots):
            put(s, amp[s])

    @pl.when(mirrored != 0)
    def _():
        for s in range(slots):
            put(s, amp[s].T)

    chunks = 4
    height = slots * n // chunks
    per = 2 * entries // chunks

    def product(v, prod, q):
        rows = slice(q * height, (q + 1) * height)
        prod[rows] = jnp.dot(
            f_pair[rows], amp_high[v], preferred_element_type=F32
        ) + jnp.dot(f_pair[rows, :n], amp_low[v], preferred_element_type=F32)

    def collect(v, prod, q):
        for e in range(q * per, (q + 1) * per):
            i, k = e // entries, e % entries
            code = codes[2 * v + i, k]
            to = pl.ds(pl.multiple_of(((code >> 8) & 15) * n, n), n)
            source = pl.ds(pl.multiple_of(((code >> 4) & 15) * n, n), n)
            new = prod[source, i * n : (i + 1) * n]
            r = code & 15
            grouped[r, to, :] = jnp.where(code >= FIRST, new, grouped[r, to, :] + new)

    for q in range(chunks):
        product(0, prod_a, q)

    def two(w, c):
        v = 2 * w
        for q in range(chunks):
            product(v + 1, prod_b, q)
            collect(v, prod_a, q)
        for q in range(chunks):
            product(v + 2, prod_a, q)
            collect(v + 1, prod_b, q)
        return c

    lax.fori_loop(0, slots // 4 - 1, two, 0)
    last = slots // 2 - 1
    for q in range(chunks):
        product(last, prod_b, q)
        collect(last - 1, prod_a, q)
    for q in range(chunks):
        collect(last, prod_b, q)

    step = 4
    for g in range(0, slots, step):

        def block(r):
            return jnp.concatenate(
                [
                    jnp.where(touched[o, r] > 0, grouped[r, o * n : (o + 1) * n, :], 0.0)
                    for o in range(g, g + step)
                ],
                axis=0,
            )

        parts = [halves(block(r)) for r in range(slots)]
        high = jnp.concatenate([a for a, _ in parts], axis=1)
        low = jnp.concatenate([b for _, b in parts], axis=1)
        both = jnp.dot(high, f_turn[...], preferred_element_type=F32)
        rest = jnp.dot(low, f_turn[:, :n], preferred_element_type=F32)
        total = both[:, :n] + both[:, n:] + rest
        out[g : g + step] = total.reshape(step, n, n)


def ladder(codes, touched, info, amp, f_pair, f_turn):
    slots, n, _ = amp.shape
    wide = slots * n
    whole = pl.BlockSpec((slots, n, n), lambda i, *_: (0, 0, 0))
    table = pl.BlockSpec((wide, 2 * n), lambda i, *_: (0, 0))
    return pl.pallas_call(
        ladder_body,
        out_shape=jax.ShapeDtypeStruct((slots, n, n), F32),
        grid_spec=pltpu.PrefetchScalarGridSpec(
            num_scalar_prefetch=3,
            grid=(1,),
            in_specs=[whole, table, table],
            out_specs=whole,
            scratch_shapes=[
                pltpu.VMEM((slots // 2, 2 * n, 2 * n), BF16),
                pltpu.VMEM((slots // 2, n, 2 * n), BF16),
                pltpu.VMEM((wide, 2 * n), F32),
                pltpu.VMEM((wide, 2 * n), F32),
                pltpu.VMEM((slots, wide, n), F32),
            ],
        ),
        compiler_params=pltpu.CompilerParams(vmem_limit_bytes=48 << 20),
        cost_estimate=pl.CostEstimate(
            flops=12 * wide * wide * n, bytes_accessed=4 << 20, transcendentals=0
        ),
        name="ladder",
    )(codes, touched, info, amp, f_pair, f_turn)


def pairs_body(spot, blocks, out, *, per_home):
    count = blocks.shape[0]
    homes = count // per_home
    half = count // 2
    out[...] = jnp.zeros(out.shape, F32)

    def one(q, c):
        row = (q % per_home) * homes + q // per_home
        value = blocks[row] + blocks[row + homes // 2]
        out[spot[q]] = value
        out[spot[q + half]] = value
        return c

    lax.fori_loop(0, half, one, 0, unroll=4)


def join_pairs(spot, blocks, own_slots, per_home):
    def body(spot, blocks, out):
        pairs_body(spot, blocks, out, per_home=per_home)

    return pl.pallas_call(
        body,
        out_shape=jax.ShapeDtypeStruct((own_slots,) + blocks.shape[1:], F32),
        grid_spec=pltpu.PrefetchScalarGridSpec(
            num_scalar_prefetch=1,
            grid=(1,),
            in_specs=[pl.BlockSpec(blocks.shape, lambda i, *_: (0, 0, 0))],
            out_specs=pl.BlockSpec((own_slots,) + blocks.shape[1:], lambda i, *_: (0, 0, 0)),
        ),
        compiler_params=pltpu.CompilerParams(vmem_limit_bytes=16 << 20),
        cost_estimate=pl.CostEstimate(flops=1 << 18, bytes_accessed=3 << 20, transcendentals=0),
        name="join_pairs",
    )(spot, blocks)


def settle(info, blocks, own_most, local_slots, n, group):
    parts = blocks.shape[0]
    per = parts // local_slots

    def body(info, src, out):
        plain = info[0]
        swap = info[1]
        first = pl.program_id(0) * group

        def as_is(g):
            for i in range(local_slots):
                out[i, g] = src[i * per : (i + 1) * per, g].reshape(n, n)

        def turned(g):
            for i in range(local_slots):
                base = jnp.where(swap != 0, local_slots - 1 - i, i) * per
                out[i, g] = src[pl.ds(base, per), g].reshape(n, n).T

        @pl.when(first + group <= plain)
        def _():
            for g in range(group):
                as_is(g)

        @pl.when(first >= plain)
        def _():
            for g in range(group):
                turned(g)

        @pl.when((first < plain) & (first + group > plain))
        def _():
            for g in range(group):
                pl.when(first + g < plain)(functools.partial(as_is, g))
                pl.when(first + g >= plain)(functools.partial(turned, g))

    return pl.pallas_call(
        body,
        out_shape=jax.ShapeDtypeStruct((local_slots, own_most, n, n), F32),
        grid_spec=pltpu.PrefetchScalarGridSpec(
            num_scalar_prefetch=1,
            grid=(own_most // group,),
            in_specs=[
                pl.BlockSpec(
                    (parts, group) + blocks.shape[2:], lambda i, *_: (0, i, 0, 0)
                )
            ],
            out_specs=pl.BlockSpec((local_slots, group, n, n), lambda i, *_: (0, i, 0, 0)),
        ),
        compiler_params=pltpu.CompilerParams(vmem_limit_bytes=16 << 20),
        cost_estimate=pl.CostEstimate(flops=1 << 18, bytes_accessed=4 << 20, transcendentals=0),
        name="settle",
    )(info, blocks)


def on_device(amplitudes, factors, integral_quadruple_table, pair_region, owner_map):
    pair_count = lax.axis_size("pair")
    virt_count = lax.axis_size("virt")
    my_pair = lax.axis_index("pair")
    my_virt = lax.axis_index("virt")
    local_slots, per_home, n, _ = amplitudes.shape
    pair_total = owner_map.shape[0]
    half = pair_total // 2
    own_most = 2 * per_home

    pair = my_pair * per_home + my_virt
    mirrored = (pair >= half).astype(jnp.int32)
    region = pair_region[pair % half]
    rows = integral_quadruple_table[region]
    o, left, right = rows[..., 0], rows[..., 1], rows[..., 2]
    partner = jnp.where(o < OFF_DIAG, o ^ 1, o)
    codes = jnp.where(
        mirrored != 0, partner * 256 + right * 16 + left, o * 256 + left * 16 + right
    )
    info = jnp.stack([region, mirrored])
    group = ((codes >> 8) * 16 + (codes & 15)).reshape(-1)
    place = jnp.arange(group.shape[0])
    met = (group[:, None] == group[None, :]) & (place[None, :] < place[:, None])
    codes = codes + jnp.where(jnp.any(met, axis=1), 0, FIRST).reshape(codes.shape)
    slot_total = codes.shape[0]
    touched = jnp.any(group[None, :] == jnp.arange(slot_total * 16)[:, None], axis=1)
    touched = touched.astype(jnp.int32).reshape(slot_total, 16)

    same = (owner_map[:, None] == owner_map[None, :]) & (
        jnp.arange(pair_total)[None, :] < jnp.arange(pair_total)[:, None]
    )
    spot = owner_map * own_most + jnp.sum(same.astype(jnp.int32), axis=1)

    plain = jnp.sum((owner_map[:half] == my_pair).astype(jnp.int32))
    swap = (my_virt * local_slots < OFF_DIAG).astype(jnp.int32)
    settle_info = jnp.stack([plain, swap])

    amp = lax.all_to_all(amplitudes, "virt", split_axis=1, concat_axis=0, tiled=True)
    f_pair, f_turn = split_factors(info, factors)
    amp, codes, touched, info, f_pair, f_turn, spot, settle_info = lax.optimization_barrier(
        (amp, codes, touched, info, f_pair, f_turn, spot, settle_info)
    )
    result = ladder(codes, touched, info, amp.reshape(-1, n, n), f_pair, f_turn)
    sheets = result.reshape(virt_count * pair_count, -1, n)
    spread = lax.all_to_all(sheets, ("virt", "pair"), split_axis=0, concat_axis=0, tiled=True)
    joined = join_pairs(spot, spread, pair_count * own_most, per_home)
    arrived = lax.all_to_all(joined, "pair", split_axis=0, concat_axis=0, tiled=True)
    return settle(
        settle_info,
        arrived.reshape(pair_count, own_most, -1, n),
        own_most,
        local_slots,
        n,
        4,
    )


def solution(mesh):
    return jax.shard_map(
        on_device,
        mesh=mesh,
        in_specs=(P("virt", "pair", None, None), P(), P(), P(), P()),
        out_specs=P("virt", "pair", None, None),
        check_vma=False,
    )
```

```python
import functools

import jax
import jax.numpy as jnp
from jax import lax
from jax.experimental import pallas as pl
from jax.experimental.pallas import tpu as pltpu
from jax.sharding import PartitionSpec as P

DOM = 4
OFF_DIAG = DOM * (DOM - 1)
F32 = jnp.float32
BF16 = jnp.bfloat16
FIRST = 1 << 12


def halves(x):
    high = x.astype(BF16)
    return high, (x - high.astype(F32)).astype(BF16)


def split_body(info, fac, f_pair, f_turn):
    slots, n = fac.shape[1], fac.shape[2]
    for l in range(slots):
        tile = fac[0, l]
        rows = slice(l * n, (l + 1) * n)
        f_pair[rows, :n], f_pair[rows, n:] = halves(tile)
        f_turn[rows, :n], f_turn[rows, n:] = halves(tile.T)


def split_factors(info, factors):
    _, slots, n, _ = factors.shape
    shape = jax.ShapeDtypeStruct((slots * n, 2 * n), BF16)
    spec = pl.BlockSpec(shape.shape, lambda i, *_: (0, 0))
    return pl.pallas_call(
        split_body,
        out_shape=[shape, shape],
        grid_spec=pltpu.PrefetchScalarGridSpec(
            num_scalar_prefetch=1,
            grid=(1,),
            in_specs=[pl.BlockSpec((1, slots, n, n), lambda i, info: (info[0], 0, 0, 0))],
            out_specs=[spec, spec],
        ),
        compiler_params=pltpu.CompilerParams(vmem_limit_bytes=16 << 20),
        cost_estimate=pl.CostEstimate(flops=1 << 20, bytes_accessed=3 << 20, transcendentals=0),
        name="split_factors",
    )(info, factors)


def ladder_body(
    codes,
    touched,
    info,
    amp,
    f_pair,
    turn_source,
    out,
    amp_high,
    amp_low,
    prod_a,
    prod_b,
    grouped,
    f_turn,
    piece,
    sems,
):
    slots, n, _ = out.shape
    entries = codes.shape[1]
    mirrored = info[1]
    fetch = pltpu.make_async_copy(turn_source, f_turn, sems.at[0])
    fetch.start()

    def put(s, tile):
        v, i = s // 2, s % 2
        high, low = halves(tile)
        amp_high[v, :n, i * n : (i + 1) * n] = high
        amp_high[v, n:, i * n : (i + 1) * n] = high
        amp_low[v, :, i * n : (i + 1) * n] = low

    @pl.when(mirrored == 0)
    def _():
        for s in range(slots):
            put(s, amp[s])

    @pl.when(mirrored != 0)
    def _():
        for s in range(slots):
            put(s, amp[s].T)

    chunks = 4
    height = slots * n // chunks
    per = 2 * entries // chunks

    def product(v, prod, q):
        rows = slice(q * height, (q + 1) * height)
        prod[rows] = jnp.dot(
            f_pair[rows], amp_high[v], preferred_element_type=F32
        ) + jnp.dot(f_pair[rows, :n], amp_low[v], preferred_element_type=F32)

    def collect(v, prod, q):
        for e in range(q * per, (q + 1) * per):
            i, k = e // entries, e % entries
            code = codes[2 * v + i, k]
            to = pl.ds(pl.multiple_of(((code >> 8) & 15) * n, n), n)
            source = pl.ds(pl.multiple_of(((code >> 4) & 15) * n, n), n)
            new = prod[source, i * n : (i + 1) * n]
            r = code & 15
            grouped[r, to, :] = jnp.where(code >= FIRST, new, grouped[r, to, :] + new)

    for q in range(chunks):
        product(0, prod_a, q)

    def two(w, c):
        v = 2 * w
        for q in range(chunks):
            product(v + 1, prod_b, q)
            collect(v, prod_a, q)
        for q in range(chunks):
            product(v + 2, prod_a, q)
            collect(v + 1, prod_b, q)
        return c

    lax.fori_loop(0, slots // 4 - 1, two, 0)
    last = slots // 2 - 1
    for q in range(chunks):
        product(last, prod_b, q)
        collect(last - 1, prod_a, q)
    for q in range(chunks):
        collect(last, prod_b, q)

    fetch.wait()
    step = slots // piece.shape[0]
    copies = []
    for g in range(0, slots, step):

        def block(r):
            return jnp.concatenate(
                [
                    jnp.where(touched[o, r] > 0, grouped[r, o * n : (o + 1) * n, :], 0.0)
                    for o in range(g, g + step)
                ],
                axis=0,
            )

        parts = [halves(block(r)) for r in range(slots)]
        high = jnp.concatenate([a for a, _ in parts], axis=1)
        low = jnp.concatenate([b for _, b in parts], axis=1)
        both = jnp.dot(high, f_turn[...], preferred_element_type=F32)
        rest = jnp.dot(low, f_turn[:, :n], preferred_element_type=F32)
        total = both[:, :n] + both[:, n:] + rest
        at = g // step
        piece[at] = total.reshape(step, n, n)
        copy = pltpu.make_async_copy(piece.at[at], out.at[pl.ds(g, step)], sems.at[1 + at])
        copy.start()
        copies.append(copy)
    for copy in copies:
        copy.wait()


def ladder(codes, touched, info, amp, f_pair, f_turn):
    slots, n, _ = amp.shape
    wide = slots * n
    whole = pl.BlockSpec((slots, n, n), lambda i, *_: (0, 0, 0))
    table = pl.BlockSpec((wide, 2 * n), lambda i, *_: (0, 0))
    return pl.pallas_call(
        ladder_body,
        out_shape=jax.ShapeDtypeStruct((slots, n, n), F32),
        grid_spec=pltpu.PrefetchScalarGridSpec(
            num_scalar_prefetch=3,
            grid=(1,),
            in_specs=[whole, table, pl.BlockSpec(memory_space=pl.ANY)],
            out_specs=pl.BlockSpec(memory_space=pl.ANY),
            scratch_shapes=[
                pltpu.VMEM((slots // 2, 2 * n, 2 * n), BF16),
                pltpu.VMEM((slots // 2, n, 2 * n), BF16),
                pltpu.VMEM((wide, 2 * n), F32),
                pltpu.VMEM((wide, 2 * n), F32),
                pltpu.VMEM((slots, wide, n), F32),
                pltpu.VMEM((wide, 2 * n), BF16),
                pltpu.VMEM((4, slots // 4, n, n), F32),
                pltpu.SemaphoreType.DMA((5,)),
            ],
        ),
        compiler_params=pltpu.CompilerParams(vmem_limit_bytes=48 << 20),
        cost_estimate=pl.CostEstimate(
            flops=12 * wide * wide * n, bytes_accessed=4 << 20, transcendentals=0
        ),
        name="ladder",
    )(codes, touched, info, amp, f_pair, f_turn)


def pairs_body(spot, blocks, out, *, per_home):
    count = blocks.shape[0]
    homes = count // per_home
    half = count // 2
    out[...] = jnp.zeros(out.shape, F32)

    def home(h, c):
        for v in range(per_home):
            row = v * homes + h
            q = h * per_home + v
            value = blocks[row] + blocks[row + homes // 2]
            out[spot[q]] = value
            out[spot[q + half]] = value
        return c

    lax.fori_loop(0, homes // 2, home, 0)


def join_pairs(spot, blocks, own_slots, per_home):
    def body(spot, blocks, out):
        pairs_body(spot, blocks, out, per_home=per_home)

    return pl.pallas_call(
        body,
        out_shape=jax.ShapeDtypeStruct((own_slots,) + blocks.shape[1:], F32),
        grid_spec=pltpu.PrefetchScalarGridSpec(
            num_scalar_prefetch=1,
            grid=(1,),
            in_specs=[pl.BlockSpec(blocks.shape, lambda i, *_: (0, 0, 0))],
            out_specs=pl.BlockSpec((own_slots,) + blocks.shape[1:], lambda i, *_: (0, 0, 0)),
        ),
        compiler_params=pltpu.CompilerParams(vmem_limit_bytes=16 << 20),
        cost_estimate=pl.CostEstimate(flops=1 << 18, bytes_accessed=3 << 20, transcendentals=0),
        name="join_pairs",
    )(spot, blocks)


def settle(info, blocks, own_most, local_slots, n, group):
    parts = blocks.shape[0]
    per = parts // local_slots

    def body(info, src, out):
        plain = info[0]
        swap = info[1]
        first = pl.program_id(0) * group

        def as_is(g):
            for i in range(local_slots):
                out[i, g] = src[i * per : (i + 1) * per, g].reshape(n, n)

        def turned(g):
            for i in range(local_slots):
                base = jnp.where(swap != 0, local_slots - 1 - i, i) * per
                out[i, g] = src[pl.ds(base, per), g].reshape(n, n).T

        @pl.when(first + group <= plain)
        def _():
            for g in range(group):
                as_is(g)

        @pl.when(first >= plain)
        def _():
            for g in range(group):
                turned(g)

        @pl.when((first < plain) & (first + group > plain))
        def _():
            for g in range(group):
                pl.when(first + g < plain)(functools.partial(as_is, g))
                pl.when(first + g >= plain)(functools.partial(turned, g))

    return pl.pallas_call(
        body,
        out_shape=jax.ShapeDtypeStruct((local_slots, own_most, n, n), F32),
        grid_spec=pltpu.PrefetchScalarGridSpec(
            num_scalar_prefetch=1,
            grid=(own_most // group,),
            in_specs=[
                pl.BlockSpec(
                    (parts, group) + blocks.shape[2:], lambda i, *_: (0, i, 0, 0)
                )
            ],
            out_specs=pl.BlockSpec((local_slots, group, n, n), lambda i, *_: (0, i, 0, 0)),
        ),
        compiler_params=pltpu.CompilerParams(vmem_limit_bytes=16 << 20),
        cost_estimate=pl.CostEstimate(flops=1 << 18, bytes_accessed=4 << 20, transcendentals=0),
        name="settle",
    )(info, blocks)


def on_device(amplitudes, factors, integral_quadruple_table, pair_region, owner_map):
    pair_count = lax.axis_size("pair")
    virt_count = lax.axis_size("virt")
    my_pair = lax.axis_index("pair")
    my_virt = lax.axis_index("virt")
    local_slots, per_home, n, _ = amplitudes.shape
    pair_total = owner_map.shape[0]
    half = pair_total // 2
    own_most = 2 * per_home

    pair = my_pair * per_home + my_virt
    mirrored = (pair >= half).astype(jnp.int32)
    region = pair_region[pair % half]
    rows = integral_quadruple_table[region]
    o, left, right = rows[..., 0], rows[..., 1], rows[..., 2]
    partner = jnp.where(o < OFF_DIAG, o ^ 1, o)
    codes = jnp.where(
        mirrored != 0, partner * 256 + right * 16 + left, o * 256 + left * 16 + right
    )
    info = jnp.stack([region, mirrored])
    group = ((codes >> 8) * 16 + (codes & 15)).reshape(-1)
    place = jnp.arange(group.shape[0])
    met = (group[:, None] == group[None, :]) & (place[None, :] < place[:, None])
    codes = codes + jnp.where(jnp.any(met, axis=1), 0, FIRST).reshape(codes.shape)
    slot_total = codes.shape[0]
    touched = jnp.any(group[None, :] == jnp.arange(slot_total * 16)[:, None], axis=1)
    touched = touched.astype(jnp.int32).reshape(slot_total, 16)

    same = (owner_map[:, None] == owner_map[None, :]) & (
        jnp.arange(pair_total)[None, :] < jnp.arange(pair_total)[:, None]
    )
    spot = owner_map * own_most + jnp.sum(same.astype(jnp.int32), axis=1)

    plain = jnp.sum((owner_map[:half] == my_pair).astype(jnp.int32))
    swap = (my_virt * local_slots < OFF_DIAG).astype(jnp.int32)
    settle_info = jnp.stack([plain, swap])

    amp = lax.all_to_all(amplitudes, "virt", split_axis=1, concat_axis=0, tiled=True)
    f_pair, f_turn = split_factors(info, factors)
    amp, codes, touched, info, f_pair, f_turn, spot, settle_info = lax.optimization_barrier(
        (amp, codes, touched, info, f_pair, f_turn, spot, settle_info)
    )
    result = ladder(codes, touched, info, amp.reshape(-1, n, n), f_pair, f_turn)
    sheets = result.reshape(virt_count * pair_count, -1, n)
    spread = lax.all_to_all(sheets, ("virt", "pair"), split_axis=0, concat_axis=0, tiled=True)
    joined = join_pairs(spot, spread, pair_count * own_most, per_home)
    arrived = lax.all_to_all(joined, "pair", split_axis=0, concat_axis=0, tiled=True)
    return settle(
        settle_info,
        arrived.reshape(pair_count, own_most, -1, n),
        own_most,
        local_slots,
        n,
        8,
    )


def solution(mesh):
    return jax.shard_map(
        on_device,
        mesh=mesh,
        in_specs=(P("virt", "pair", None, None), P(), P(), P(), P()),
        out_specs=P("virt", "pair", None, None),
        check_vma=False,
    )
```

```python
import functools

import jax
import jax.numpy as jnp
from jax import lax
from jax.experimental import pallas as pl
from jax.experimental.pallas import tpu as pltpu
from jax.sharding import PartitionSpec as P

DOM = 4
OFF_DIAG = DOM * (DOM - 1)
F32 = jnp.float32
BF16 = jnp.bfloat16
FIRST = 1 << 12


def halves(x):
    high = x.astype(BF16)
    return high, (x - high.astype(F32)).astype(BF16)


def split_body(info, fac, f_pair, f_turn):
    slots, n = fac.shape[1], fac.shape[2]
    for l in range(slots):
        tile = fac[0, l]
        rows = slice(l * n, (l + 1) * n)
        f_pair[rows, :n], f_pair[rows, n:] = halves(tile)
        f_turn[rows, :n], f_turn[rows, n:] = halves(tile.T)


def split_factors(info, factors):
    _, slots, n, _ = factors.shape
    shape = jax.ShapeDtypeStruct((slots * n, 2 * n), BF16)
    spec = pl.BlockSpec(shape.shape, lambda i, *_: (0, 0))
    return pl.pallas_call(
        split_body,
        out_shape=[shape, shape],
        grid_spec=pltpu.PrefetchScalarGridSpec(
            num_scalar_prefetch=1,
            grid=(1,),
            in_specs=[pl.BlockSpec((1, slots, n, n), lambda i, info: (info[0], 0, 0, 0))],
            out_specs=[spec, spec],
        ),
        compiler_params=pltpu.CompilerParams(vmem_limit_bytes=16 << 20),
        cost_estimate=pl.CostEstimate(flops=1 << 20, bytes_accessed=3 << 20, transcendentals=0),
        name="split_factors",
    )(info, factors)


def deal_body(info, source, *refs):
    outs, held, sems = refs[:-2], refs[-2], refs[-1]
    count = len(outs)
    local = source.shape[0]
    taken, given = [], []
    for d, out in enumerate(outs):
        to = lax.rem(info[2] + d, count)
        taken.append(
            [
                pltpu.make_async_copy(source.at[i, to], held.at[d, i], sems.at[d, i])
                for i in range(local)
            ]
        )
        given.append(pltpu.make_async_copy(held.at[d], out, sems.at[d, local]))
    for copies in taken:
        for copy in copies:
            copy.start()
    for copies, copy in zip(taken, given):
        for each in copies:
            each.wait()
        copy.start()
    for copy in given:
        copy.wait()


def deal(info, amplitudes):
    local, count, n, _ = amplitudes.shape
    anywhere = pl.BlockSpec(memory_space=pl.ANY)
    return pl.pallas_call(
        deal_body,
        out_shape=[jax.ShapeDtypeStruct((local, n, n), F32)] * count,
        grid_spec=pltpu.PrefetchScalarGridSpec(
            num_scalar_prefetch=1,
            grid=(1,),
            in_specs=[anywhere],
            out_specs=[anywhere] * count,
            scratch_shapes=[
                pltpu.VMEM((count, local, n, n), F32),
                pltpu.SemaphoreType.DMA((count, local + 1)),
            ],
        ),
        compiler_params=pltpu.CompilerParams(vmem_limit_bytes=56 << 20),
        cost_estimate=pl.CostEstimate(flops=0, bytes_accessed=2 << 20, transcendentals=0),
        name="deal",
    )(info, amplitudes)


def ladder_body(
    codes, touched, info, *refs
):
    f_pair, f_turn, out, amp_high, amp_low, prod_a, prod_b, grouped = refs[-8:]
    amps = refs[:-8]
    slots, n, _ = out.shape
    entries = codes.shape[1]
    mirrored = info[1]

    def put(v, i, tile):
        high, low = halves(tile)
        amp_high[v, :n, i * n : (i + 1) * n] = high
        amp_high[v, n:, i * n : (i + 1) * n] = high
        amp_low[v, :, i * n : (i + 1) * n] = low

    count = len(amps)
    origins = [lax.rem(info[2] + (count - d), count) for d in range(count)]

    @pl.when(mirrored == 0)
    def _():
        for v, amp in zip(origins, amps):
            for i in range(amp.shape[0]):
                put(v, i, amp[i])

    @pl.when(mirrored != 0)
    def _():
        for v, amp in zip(origins, amps):
            for i in range(amp.shape[0]):
                put(v, i, amp[i].T)

    chunks = 4
    height = slots * n // chunks
    per = 2 * entries // chunks

    def product(v, prod, q):
        rows = slice(q * height, (q + 1) * height)
        prod[rows] = jnp.dot(
            f_pair[rows], amp_high[v], preferred_element_type=F32
        ) + jnp.dot(f_pair[rows, :n], amp_low[v], preferred_element_type=F32)

    def collect(v, prod, q):
        for e in range(q * per, (q + 1) * per):
            i, k = e // entries, e % entries
            code = codes[2 * v + i, k]
            to = pl.ds(pl.multiple_of(((code >> 8) & 15) * n, n), n)
            source = pl.ds(pl.multiple_of(((code >> 4) & 15) * n, n), n)
            new = prod[source, i * n : (i + 1) * n]
            r = code & 15
            grouped[r, to, :] = jnp.where(code >= FIRST, new, grouped[r, to, :] + new)

    for q in range(chunks):
        product(0, prod_a, q)

    def two(w, c):
        v = 2 * w
        for q in range(chunks):
            product(v + 1, prod_b, q)
            collect(v, prod_a, q)
        for q in range(chunks):
            product(v + 2, prod_a, q)
            collect(v + 1, prod_b, q)
        return c

    lax.fori_loop(0, slots // 4 - 1, two, 0)
    last = slots // 2 - 1
    for q in range(chunks):
        product(last, prod_b, q)
        collect(last - 1, prod_a, q)
    for q in range(chunks):
        collect(last, prod_b, q)

    step = 4
    for g in range(0, slots, step):

        def block(r):
            return jnp.concatenate(
                [
                    jnp.where(touched[o, r] > 0, grouped[r, o * n : (o + 1) * n, :], 0.0)
                    for o in range(g, g + step)
                ],
                axis=0,
            )

        parts = [halves(block(r)) for r in range(slots)]
        high = jnp.concatenate([a for a, _ in parts], axis=1)
        low = jnp.concatenate([b for _, b in parts], axis=1)
        both = jnp.dot(high, f_turn[...], preferred_element_type=F32)
        rest = jnp.dot(low, f_turn[:, :n], preferred_element_type=F32)
        total = both[:, :n] + both[:, n:] + rest
        out[g : g + step] = total.reshape(step, n, n)


def ladder(codes, touched, info, amps, f_pair, f_turn):
    local, n, _ = amps[0].shape
    slots = local * len(amps)
    wide = slots * n
    few = pl.BlockSpec((local, n, n), lambda i, *_: (0, 0, 0))
    whole = pl.BlockSpec((slots, n, n), lambda i, *_: (0, 0, 0))
    table = pl.BlockSpec((wide, 2 * n), lambda i, *_: (0, 0))
    return pl.pallas_call(
        ladder_body,
        out_shape=jax.ShapeDtypeStruct((slots, n, n), F32),
        grid_spec=pltpu.PrefetchScalarGridSpec(
            num_scalar_prefetch=3,
            grid=(1,),
            in_specs=[few] * len(amps) + [table, table],
            out_specs=whole,
            scratch_shapes=[
                pltpu.VMEM((slots // 2, 2 * n, 2 * n), BF16),
                pltpu.VMEM((slots // 2, n, 2 * n), BF16),
                pltpu.VMEM((wide, 2 * n), F32),
                pltpu.VMEM((wide, 2 * n), F32),
                pltpu.VMEM((slots, wide, n), F32),
            ],
        ),
        compiler_params=pltpu.CompilerParams(vmem_limit_bytes=48 << 20),
        cost_estimate=pl.CostEstimate(
            flops=12 * wide * wide * n, bytes_accessed=4 << 20, transcendentals=0
        ),
        name="ladder",
    )(codes, touched, info, *amps, f_pair, f_turn)


def pairs_body(spot, blocks, out, *, per_home):
    count = blocks.shape[0]
    homes = count // per_home
    half = count // 2
    out[...] = jnp.zeros(out.shape, F32)

    def home(h, c):
        for v in range(per_home):
            row = v * homes + h
            q = h * per_home + v
            value = blocks[row] + blocks[row + homes // 2]
            out[spot[q]] = value
            out[spot[q + half]] = value
        return c

    lax.fori_loop(0, homes // 2, home, 0)


def join_pairs(spot, blocks, own_slots, per_home):
    def body(spot, blocks, out):
        pairs_body(spot, blocks, out, per_home=per_home)

    return pl.pallas_call(
        body,
        out_shape=jax.ShapeDtypeStruct((own_slots,) + blocks.shape[1:], F32),
        grid_spec=pltpu.PrefetchScalarGridSpec(
            num_scalar_prefetch=1,
            grid=(1,),
            in_specs=[pl.BlockSpec(blocks.shape, lambda i, *_: (0, 0, 0))],
            out_specs=pl.BlockSpec((own_slots,) + blocks.shape[1:], lambda i, *_: (0, 0, 0)),
        ),
        compiler_params=pltpu.CompilerParams(vmem_limit_bytes=16 << 20),
        cost_estimate=pl.CostEstimate(flops=1 << 18, bytes_accessed=3 << 20, transcendentals=0),
        name="join_pairs",
    )(spot, blocks)


def settle(info, blocks, own_most, local_slots, n, group):
    parts = blocks.shape[0]
    per = parts // local_slots

    def body(info, src, out):
        plain = info[0]
        swap = info[1]
        first = pl.program_id(0) * group

        def as_is(g):
            for i in range(local_slots):
                out[i, g] = src[i * per : (i + 1) * per, g].reshape(n, n)

        def turned(g):
            for i in range(local_slots):
                base = jnp.where(swap != 0, local_slots - 1 - i, i) * per
                out[i, g] = src[pl.ds(base, per), g].reshape(n, n).T

        @pl.when(first + group <= plain)
        def _():
            for g in range(group):
                as_is(g)

        @pl.when(first >= plain)
        def _():
            for g in range(group):
                turned(g)

        @pl.when((first < plain) & (first + group > plain))
        def _():
            for g in range(group):
                pl.when(first + g < plain)(functools.partial(as_is, g))
                pl.when(first + g >= plain)(functools.partial(turned, g))

    return pl.pallas_call(
        body,
        out_shape=jax.ShapeDtypeStruct((local_slots, own_most, n, n), F32),
        grid_spec=pltpu.PrefetchScalarGridSpec(
            num_scalar_prefetch=1,
            grid=(own_most // group,),
            in_specs=[
                pl.BlockSpec(
                    (parts, group) + blocks.shape[2:], lambda i, *_: (0, i, 0, 0)
                )
            ],
            out_specs=pl.BlockSpec((local_slots, group, n, n), lambda i, *_: (0, i, 0, 0)),
        ),
        compiler_params=pltpu.CompilerParams(vmem_limit_bytes=16 << 20),
        cost_estimate=pl.CostEstimate(flops=1 << 18, bytes_accessed=4 << 20, transcendentals=0),
        name="settle",
    )(info, blocks)


def on_device(amplitudes, factors, integral_quadruple_table, pair_region, owner_map):
    pair_count = lax.axis_size("pair")
    virt_count = lax.axis_size("virt")
    my_pair = lax.axis_index("pair")
    my_virt = lax.axis_index("virt")
    local_slots, per_home, n, _ = amplitudes.shape
    pair_total = owner_map.shape[0]
    half = pair_total // 2
    own_most = 2 * per_home

    pair = my_pair * per_home + my_virt
    mirrored = (pair >= half).astype(jnp.int32)
    region = pair_region[pair % half]
    rows = integral_quadruple_table[region]
    o, left, right = rows[..., 0], rows[..., 1], rows[..., 2]
    partner = jnp.where(o < OFF_DIAG, o ^ 1, o)
    codes = jnp.where(
        mirrored != 0, partner * 256 + right * 16 + left, o * 256 + left * 16 + right
    )
    info = jnp.stack([region, mirrored, my_virt])
    group = ((codes >> 8) * 16 + (codes & 15)).reshape(-1)
    place = jnp.arange(group.shape[0])
    met = (group[:, None] == group[None, :]) & (place[None, :] < place[:, None])
    codes = codes + jnp.where(jnp.any(met, axis=1), 0, FIRST).reshape(codes.shape)
    slot_total = codes.shape[0]
    touched = jnp.any(group[None, :] == jnp.arange(slot_total * 16)[:, None], axis=1)
    touched = touched.astype(jnp.int32).reshape(slot_total, 16)

    same = (owner_map[:, None] == owner_map[None, :]) & (
        jnp.arange(pair_total)[None, :] < jnp.arange(pair_total)[:, None]
    )
    spot = owner_map * own_most + jnp.sum(same.astype(jnp.int32), axis=1)

    plain = jnp.sum((owner_map[:half] == my_pair).astype(jnp.int32))
    swap = (my_virt * local_slots < OFF_DIAG).astype(jnp.int32)
    settle_info = jnp.stack([plain, swap])

    pieces = deal(jnp.stack([my_virt] * 3), amplitudes)
    amps = {0: pieces[0]}
    for d in sorted(range(1, virt_count), key=lambda d: -min(d, virt_count - d)):
        route = [(i, (i + d) % virt_count) for i in range(virt_count)]
        amps[d] = lax.ppermute(pieces[d], "virt", route)
    amps = [amps[d] for d in range(virt_count)]
    f_pair, f_turn = split_factors(info, factors)
    amps, codes, touched, info, f_pair, f_turn, spot, settle_info = lax.optimization_barrier(
        (amps, codes, touched, info, f_pair, f_turn, spot, settle_info)
    )
    result = ladder(codes, touched, info, amps, f_pair, f_turn)
    sheets = result.reshape(virt_count * pair_count, -1, n)
    spread = lax.all_to_all(sheets, ("virt", "pair"), split_axis=0, concat_axis=0, tiled=True)
    joined = join_pairs(spot, spread, pair_count * own_most, per_home)
    arrived = lax.all_to_all(joined, "pair", split_axis=0, concat_axis=0, tiled=True)
    return settle(
        settle_info,
        arrived.reshape(pair_count, own_most, -1, n),
        own_most,
        local_slots,
        n,
        8,
    )


def solution(mesh):
    return jax.shard_map(
        on_device,
        mesh=mesh,
        in_specs=(P("virt", "pair", None, None), P(), P(), P(), P()),
        out_specs=P("virt", "pair", None, None),
        check_vma=False,
    )
```

```python
import functools

import jax
import jax.numpy as jnp
from jax import lax
from jax.experimental import pallas as pl
from jax.experimental.pallas import tpu as pltpu
from jax.sharding import PartitionSpec as P

DOM = 4
OFF_DIAG = DOM * (DOM - 1)
F32 = jnp.float32
BF16 = jnp.bfloat16
FIRST = 1 << 12


def halves(x):
    high = x.astype(BF16)
    return high, (x - high.astype(F32)).astype(BF16)


def split_body(fac, f_pair, f_turn):
    slots, n, _ = fac.shape
    for l in range(slots):
        tile = fac[l]
        rows = slice(l * n, (l + 1) * n)
        f_pair[rows, :n], f_pair[rows, n:] = halves(tile)
        f_turn[rows, :n], f_turn[rows, n:] = halves(tile.T)


def split_factors(factors):
    slots, n, _ = factors.shape
    shape = jax.ShapeDtypeStruct((slots * n, 2 * n), BF16)
    spec = pl.BlockSpec(shape.shape, lambda i: (0, 0))
    return pl.pallas_call(
        split_body,
        out_shape=[shape, shape],
        grid=(1,),
        in_specs=[pl.BlockSpec((slots, n, n), lambda i: (0, 0, 0))],
        out_specs=[spec, spec],
        compiler_params=pltpu.CompilerParams(vmem_limit_bytes=16 << 20),
        cost_estimate=pl.CostEstimate(flops=1 << 20, bytes_accessed=3 << 20, transcendentals=0),
        name="split_factors",
    )(factors)


def deal_body(source, *refs):
    outs, held, sems = refs[:-2], refs[-2], refs[-1]
    count = len(outs)
    local = source.shape[0]
    taken, given = [], []
    for d, out in enumerate(outs):
        to = lax.rem(lax.axis_index("virt") + d, count)
        taken.append(
            [
                pltpu.make_async_copy(source.at[i, to], held.at[d, i], sems.at[d, i])
                for i in range(local)
            ]
        )
        given.append(pltpu.make_async_copy(held.at[d], out, sems.at[d, local]))
    for copies in taken:
        for copy in copies:
            copy.start()
    for copies, copy in zip(taken, given):
        for each in copies:
            each.wait()
        copy.start()
    for copy in given:
        copy.wait()


def deal(amplitudes):
    local, count, n, _ = amplitudes.shape
    anywhere = pl.BlockSpec(memory_space=pl.ANY)
    return pl.pallas_call(
        deal_body,
        out_shape=[jax.ShapeDtypeStruct((local, n, n), F32)] * count,
        in_specs=[anywhere],
        out_specs=[anywhere] * count,
        scratch_shapes=[
            pltpu.VMEM((count, local, n, n), F32),
            pltpu.SemaphoreType.DMA((count, local + 1)),
        ],
        compiler_params=pltpu.CompilerParams(vmem_limit_bytes=56 << 20),
        cost_estimate=pl.CostEstimate(flops=0, bytes_accessed=2 << 20, transcendentals=0),
        name="deal",
    )(amplitudes)


def ladder_body(
    codes, touched, *refs
):
    f_pair, f_turn, out, amp_high, amp_low, prod_a, prod_b, grouped = refs[-8:]
    amps = refs[:-8]
    slots, n, _ = out.shape
    entries = codes.shape[1]
    mirrored = (lax.axis_index("pair") >= lax.axis_size("pair") // 2).astype(jnp.int32)

    def put(v, i, tile):
        high, low = halves(tile)
        amp_high[v, :n, i * n : (i + 1) * n] = high
        amp_high[v, n:, i * n : (i + 1) * n] = high
        amp_low[v, :, i * n : (i + 1) * n] = low

    count = len(amps)
    origins = [lax.rem(lax.axis_index("virt") + (count - d), count) for d in range(count)]

    @pl.when(mirrored == 0)
    def _():
        for v, amp in zip(origins, amps):
            for i in range(amp.shape[0]):
                put(v, i, amp[i])

    @pl.when(mirrored != 0)
    def _():
        for v, amp in zip(origins, amps):
            for i in range(amp.shape[0]):
                put(v, i, amp[i].T)

    chunks = 4
    height = slots * n // chunks
    per = 2 * entries // chunks

    def product(v, prod, q):
        rows = slice(q * height, (q + 1) * height)
        prod[rows] = jnp.dot(
            f_pair[rows], amp_high[v], preferred_element_type=F32
        ) + jnp.dot(f_pair[rows, :n], amp_low[v], preferred_element_type=F32)

    def collect(v, prod, q):
        for e in range(q * per, (q + 1) * per):
            i, k = e // entries, e % entries
            code = codes[2 * v + i, k]
            to = pl.ds(pl.multiple_of(((code >> 8) & 15) * n, n), n)
            source = pl.ds(pl.multiple_of(((code >> 4) & 15) * n, n), n)
            new = prod[source, i * n : (i + 1) * n]
            r = code & 15
            grouped[r, to, :] = jnp.where(code >= FIRST, new, grouped[r, to, :] + new)

    for q in range(chunks):
        product(0, prod_a, q)

    def two(w, c):
        v = 2 * w
        for q in range(chunks):
            product(v + 1, prod_b, q)
            collect(v, prod_a, q)
        for q in range(chunks):
            product(v + 2, prod_a, q)
            collect(v + 1, prod_b, q)
        return c

    lax.fori_loop(0, slots // 4 - 1, two, 0)
    last = slots // 2 - 1
    for q in range(chunks):
        product(last, prod_b, q)
        collect(last - 1, prod_a, q)
    for q in range(chunks):
        collect(last, prod_b, q)

    step = 4
    for g in range(0, slots, step):

        def block(r):
            return jnp.concatenate(
                [
                    jnp.where(touched[o, r] > 0, grouped[r, o * n : (o + 1) * n, :], 0.0)
                    for o in range(g, g + step)
                ],
                axis=0,
            )

        parts = [halves(block(r)) for r in range(slots)]
        high = jnp.concatenate([a for a, _ in parts], axis=1)
        low = jnp.concatenate([b for _, b in parts], axis=1)
        both = jnp.dot(high, f_turn[...], preferred_element_type=F32)
        rest = jnp.dot(low, f_turn[:, :n], preferred_element_type=F32)
        total = both[:, :n] + both[:, n:] + rest
        out[g : g + step] = total.reshape(step, n, n)


def ladder(codes, touched, amps, f_pair, f_turn):
    local, n, _ = amps[0].shape
    slots = local * len(amps)
    wide = slots * n
    few = pl.BlockSpec((local, n, n), lambda i, *_: (0, 0, 0))
    whole = pl.BlockSpec((slots, n, n), lambda i, *_: (0, 0, 0))
    table = pl.BlockSpec((wide, 2 * n), lambda i, *_: (0, 0))
    return pl.pallas_call(
        ladder_body,
        out_shape=jax.ShapeDtypeStruct((slots, n, n), F32),
        grid_spec=pltpu.PrefetchScalarGridSpec(
            num_scalar_prefetch=2,
            grid=(1,),
            in_specs=[few] * len(amps) + [table, table],
            out_specs=whole,
            scratch_shapes=[
                pltpu.VMEM((slots // 2, 2 * n, 2 * n), BF16),
                pltpu.VMEM((slots // 2, n, 2 * n), BF16),
                pltpu.VMEM((wide, 2 * n), F32),
                pltpu.VMEM((wide, 2 * n), F32),
                pltpu.VMEM((slots, wide, n), F32),
            ],
        ),
        compiler_params=pltpu.CompilerParams(vmem_limit_bytes=48 << 20),
        cost_estimate=pl.CostEstimate(
            flops=12 * wide * wide * n, bytes_accessed=4 << 20, transcendentals=0
        ),
        name="ladder",
    )(codes, touched, *amps, f_pair, f_turn)


def pairs_body(spot, blocks, out, *, per_home):
    count = blocks.shape[0]
    homes = count // per_home
    half = count // 2
    out[...] = jnp.zeros(out.shape, F32)

    def home(h, c):
        for v in range(per_home):
            row = v * homes + h
            q = h * per_home + v
            value = blocks[row] + blocks[row + homes // 2]
            out[spot[q]] = value
            out[spot[q + half]] = value
        return c

    lax.fori_loop(0, homes // 2, home, 0)


def join_pairs(spot, blocks, own_slots, per_home):
    def body(spot, blocks, out):
        pairs_body(spot, blocks, out, per_home=per_home)

    return pl.pallas_call(
        body,
        out_shape=jax.ShapeDtypeStruct((own_slots,) + blocks.shape[1:], F32),
        grid_spec=pltpu.PrefetchScalarGridSpec(
            num_scalar_prefetch=1,
            grid=(1,),
            in_specs=[pl.BlockSpec(blocks.shape, lambda i, *_: (0, 0, 0))],
            out_specs=pl.BlockSpec((own_slots,) + blocks.shape[1:], lambda i, *_: (0, 0, 0)),
        ),
        compiler_params=pltpu.CompilerParams(vmem_limit_bytes=16 << 20),
        cost_estimate=pl.CostEstimate(flops=1 << 18, bytes_accessed=3 << 20, transcendentals=0),
        name="join_pairs",
    )(spot, blocks)


def settle(held, blocks, own_most, local_slots, n, group):
    parts = blocks.shape[0]
    per = parts // local_slots

    def body(held, src, out):
        plain = held[0]
        swap = (lax.axis_index("virt") * local_slots < OFF_DIAG).astype(jnp.int32)
        first = pl.program_id(0) * group

        def as_is(g):
            for i in range(local_slots):
                out[i, g] = src[i * per : (i + 1) * per, g].reshape(n, n)

        def turned(g):
            for i in range(local_slots):
                base = jnp.where(swap != 0, local_slots - 1 - i, i) * per
                out[i, g] = src[pl.ds(base, per), g].reshape(n, n).T

        @pl.when(first + group <= plain)
        def _():
            for g in range(group):
                as_is(g)

        @pl.when(first >= plain)
        def _():
            for g in range(group):
                turned(g)

        @pl.when((first < plain) & (first + group > plain))
        def _():
            for g in range(group):
                pl.when(first + g < plain)(functools.partial(as_is, g))
                pl.when(first + g >= plain)(functools.partial(turned, g))

    return pl.pallas_call(
        body,
        out_shape=jax.ShapeDtypeStruct((local_slots, own_most, n, n), F32),
        grid_spec=pltpu.PrefetchScalarGridSpec(
            num_scalar_prefetch=1,
            grid=(own_most // group,),
            in_specs=[
                pl.BlockSpec(
                    (parts, group) + blocks.shape[2:], lambda i, *_: (0, i, 0, 0)
                )
            ],
            out_specs=pl.BlockSpec((local_slots, group, n, n), lambda i, *_: (0, i, 0, 0)),
        ),
        compiler_params=pltpu.CompilerParams(vmem_limit_bytes=16 << 20),
        cost_estimate=pl.CostEstimate(flops=1 << 18, bytes_accessed=4 << 20, transcendentals=0),
        name="settle",
    )(held, blocks)


def on_device(amplitudes, factors, integral_quadruple_table, pair_region, owner_map):
    pair_count = lax.axis_size("pair")
    virt_count = lax.axis_size("virt")
    my_pair = lax.axis_index("pair")
    my_virt = lax.axis_index("virt")
    local_slots, per_home, n, _ = amplitudes.shape
    pair_total = owner_map.shape[0]
    half = pair_total // 2
    own_most = 2 * per_home

    pair = my_pair * per_home + my_virt
    mirrored = (pair >= half).astype(jnp.int32)
    region = pair_region[pair % half]
    rows = integral_quadruple_table[region]
    o, left, right = rows[..., 0], rows[..., 1], rows[..., 2]
    partner = jnp.where(o < OFF_DIAG, o ^ 1, o)
    codes = jnp.where(
        mirrored != 0, partner * 256 + right * 16 + left, o * 256 + left * 16 + right
    )
    group = ((codes >> 8) * 16 + (codes & 15)).reshape(-1)
    place = jnp.arange(group.shape[0])
    met = (group[:, None] == group[None, :]) & (place[None, :] < place[:, None])
    codes = codes + jnp.where(jnp.any(met, axis=1), 0, FIRST).reshape(codes.shape)
    slot_total = codes.shape[0]
    touched = jnp.any(group[None, :] == jnp.arange(slot_total * 16)[:, None], axis=1)
    touched = touched.astype(jnp.int32).reshape(slot_total, 16)

    same = (owner_map[:, None] == owner_map[None, :]) & (
        jnp.arange(pair_total)[None, :] < jnp.arange(pair_total)[:, None]
    )
    spot = owner_map * own_most + jnp.sum(same.astype(jnp.int32), axis=1)

    plain = jnp.sum((owner_map[:half] == my_pair).astype(jnp.int32))
    held = plain.reshape(1)

    pieces = deal(amplitudes)
    amps = {0: pieces[0]}
    for d in sorted(range(1, virt_count), key=lambda d: -min(d, virt_count - d)):
        route = [(i, (i + d) % virt_count) for i in range(virt_count)]
        amps[d] = lax.ppermute(pieces[d], "virt", route)
    amps = [amps[d] for d in range(virt_count)]
    f_pair, f_turn = split_factors(lax.dynamic_index_in_dim(factors, region, 0, keepdims=False))
    amps, codes, touched, f_pair, f_turn, spot, held = lax.optimization_barrier(
        (amps, codes, touched, f_pair, f_turn, spot, held)
    )
    result = ladder(codes, touched, amps, f_pair, f_turn)
    sheets = result.reshape(virt_count * pair_count, -1, n)
    spread = lax.all_to_all(sheets, ("virt", "pair"), split_axis=0, concat_axis=0, tiled=True)
    joined = join_pairs(spot, spread, pair_count * own_most, per_home)
    arrived = lax.all_to_all(joined, "pair", split_axis=0, concat_axis=0, tiled=True)
    return settle(
        held,
        arrived.reshape(pair_count, own_most, -1, n),
        own_most,
        local_slots,
        n,
        8,
    )


def solution(mesh):
    return jax.shard_map(
        on_device,
        mesh=mesh,
        in_specs=(P("virt", "pair", None, None), P(), P(), P(), P()),
        out_specs=P("virt", "pair", None, None),
        check_vma=False,
    )
```

```python
import functools

import jax
import jax.numpy as jnp
from jax import lax
from jax.experimental import pallas as pl
from jax.experimental.pallas import tpu as pltpu
from jax.sharding import PartitionSpec as P

DOM = 4
OFF_DIAG = DOM * (DOM - 1)
F32 = jnp.float32
BF16 = jnp.bfloat16
FIRST = 1 << 12


def halves(x):
    high = x.astype(BF16)
    return high, (x - high.astype(F32)).astype(BF16)


def split_body(fac, f_pair, f_turn):
    slots, n, _ = fac.shape
    for l in range(slots):
        tile = fac[l]
        rows = slice(l * n, (l + 1) * n)
        f_pair[rows, :n], f_pair[rows, n:] = halves(tile)
        f_turn[rows, :n], f_turn[rows, n:] = halves(tile.T)


def split_factors(factors):
    slots, n, _ = factors.shape
    shape = jax.ShapeDtypeStruct((slots * n, 2 * n), BF16)
    spec = pl.BlockSpec(shape.shape, lambda i: (0, 0))
    return pl.pallas_call(
        split_body,
        out_shape=[shape, shape],
        grid=(1,),
        in_specs=[pl.BlockSpec((slots, n, n), lambda i: (0, 0, 0))],
        out_specs=[spec, spec],
        compiler_params=pltpu.CompilerParams(vmem_limit_bytes=16 << 20),
        cost_estimate=pl.CostEstimate(flops=1 << 20, bytes_accessed=3 << 20, transcendentals=0),
        name="split_factors",
    )(factors)


def deal_body(source, *refs):
    outs, held, sems = refs[:-2], refs[-2], refs[-1]
    count = len(outs)
    local = source.shape[0]
    taken, given = [], []
    for d, out in enumerate(outs):
        to = lax.rem(lax.axis_index("virt") + d, count)
        taken.append(
            [
                pltpu.make_async_copy(source.at[i, to], held.at[d, i], sems.at[d, i])
                for i in range(local)
            ]
        )
        given.append(pltpu.make_async_copy(held.at[d], out, sems.at[d, local]))
    for copies in taken:
        for copy in copies:
            copy.start()
    for copies, copy in zip(taken, given):
        for each in copies:
            each.wait()
        copy.start()
    for copy in given:
        copy.wait()


def deal(amplitudes):
    local, count, n, _ = amplitudes.shape
    anywhere = pl.BlockSpec(memory_space=pl.ANY)
    return pl.pallas_call(
        deal_body,
        out_shape=[jax.ShapeDtypeStruct((local, n, n), F32)] * count,
        in_specs=[anywhere],
        out_specs=[anywhere] * count,
        scratch_shapes=[
            pltpu.VMEM((count, local, n, n), F32),
            pltpu.SemaphoreType.DMA((count, local + 1)),
        ],
        compiler_params=pltpu.CompilerParams(vmem_limit_bytes=56 << 20),
        cost_estimate=pl.CostEstimate(flops=0, bytes_accessed=2 << 20, transcendentals=0),
        name="deal",
    )(amplitudes)


def ladder_body(
    codes, touched, *refs
):
    f_pair, f_turn, out, amp_high, amp_low, prod_a, prod_b, grouped = refs[-8:]
    amps = refs[:-8]
    slots, n, _ = out.shape
    entries = codes.shape[1]
    mirrored = (lax.axis_index("pair") >= lax.axis_size("pair") // 2).astype(jnp.int32)

    def put(v, i, tile):
        high, low = halves(tile)
        amp_high[v, :n, i * n : (i + 1) * n] = high
        amp_high[v, n:, i * n : (i + 1) * n] = high
        amp_low[v, :, i * n : (i + 1) * n] = low

    count = len(amps)
    origins = [lax.rem(lax.axis_index("virt") + (count - d), count) for d in range(count)]

    @pl.when(mirrored == 0)
    def _():
        for v, amp in zip(origins, amps):
            for i in range(amp.shape[0]):
                put(v, i, amp[i])

    @pl.when(mirrored != 0)
    def _():
        for v, amp in zip(origins, amps):
            for i in range(amp.shape[0]):
                put(v, i, amp[i].T)

    chunks = 4
    height = slots * n // chunks
    per = 2 * entries // chunks

    def product(v, prod, q):
        rows = slice(q * height, (q + 1) * height)
        prod[rows] = jnp.dot(
            f_pair[rows], amp_high[v], preferred_element_type=F32
        ) + jnp.dot(f_pair[rows, :n], amp_low[v], preferred_element_type=F32)

    def collect(v, prod, q):
        for e in range(q * per, (q + 1) * per):
            i, k = e // entries, e % entries
            code = codes[2 * v + i, k]
            to = pl.ds(pl.multiple_of(((code >> 8) & 15) * n, n), n)
            source = pl.ds(pl.multiple_of(((code >> 4) & 15) * n, n), n)
            new = prod[source, i * n : (i + 1) * n]
            r = code & 15
            grouped[r, to, :] = jnp.where(code >= FIRST, new, grouped[r, to, :] + new)

    for q in range(chunks):
        product(0, prod_a, q)

    def two(w, c):
        v = 2 * w
        for q in range(chunks):
            product(v + 1, prod_b, q)
            collect(v, prod_a, q)
        for q in range(chunks):
            product(v + 2, prod_a, q)
            collect(v + 1, prod_b, q)
        return c

    lax.fori_loop(0, slots // 4 - 1, two, 0)
    last = slots // 2 - 1
    for q in range(chunks):
        product(last, prod_b, q)
        collect(last - 1, prod_a, q)
    for q in range(chunks):
        collect(last, prod_b, q)

    step = 4
    for g in range(0, slots, step):

        def block(r):
            return jnp.concatenate(
                [
                    jnp.where(touched[o, r] > 0, grouped[r, o * n : (o + 1) * n, :], 0.0)
                    for o in range(g, g + step)
                ],
                axis=0,
            )

        parts = [halves(block(r)) for r in range(slots)]
        high = jnp.concatenate([a for a, _ in parts], axis=1)
        low = jnp.concatenate([b for _, b in parts], axis=1)
        both = jnp.dot(high, f_turn[...], preferred_element_type=F32)
        rest = jnp.dot(low, f_turn[:, :n], preferred_element_type=F32)
        total = both[:, :n] + both[:, n:] + rest
        out[g : g + step] = total.reshape(step, n, n)


def ladder(codes, touched, amps, f_pair, f_turn):
    local, n, _ = amps[0].shape
    slots = local * len(amps)
    wide = slots * n
    few = pl.BlockSpec((local, n, n), lambda i, *_: (0, 0, 0))
    whole = pl.BlockSpec((slots, n, n), lambda i, *_: (0, 0, 0))
    table = pl.BlockSpec((wide, 2 * n), lambda i, *_: (0, 0))
    return pl.pallas_call(
        ladder_body,
        out_shape=jax.ShapeDtypeStruct((slots, n, n), F32),
        grid_spec=pltpu.PrefetchScalarGridSpec(
            num_scalar_prefetch=2,
            grid=(1,),
            in_specs=[few] * len(amps) + [table, table],
            out_specs=whole,
            scratch_shapes=[
                pltpu.VMEM((slots // 2, 2 * n, 2 * n), BF16),
                pltpu.VMEM((slots // 2, n, 2 * n), BF16),
                pltpu.VMEM((wide, 2 * n), F32),
                pltpu.VMEM((wide, 2 * n), F32),
                pltpu.VMEM((slots, wide, n), F32),
            ],
        ),
        compiler_params=pltpu.CompilerParams(vmem_limit_bytes=48 << 20),
        cost_estimate=pl.CostEstimate(
            flops=12 * wide * wide * n, bytes_accessed=4 << 20, transcendentals=0
        ),
        name="ladder",
    )(codes, touched, *amps, f_pair, f_turn)


def pairs_body(spot, blocks, out, *, per_home):
    count = blocks.shape[0]
    homes = count // per_home
    half = count // 2
    out[...] = jnp.zeros(out.shape, F32)

    def home(h, c):
        for v in range(per_home):
            row = v * homes + h
            q = h * per_home + v
            value = blocks[row] + blocks[row + homes // 2]
            out[spot[q]] = value
            out[spot[q + half]] = value
        return c

    lax.fori_loop(0, homes // 2, home, 0)


def join_pairs(spot, blocks, own_slots, per_home):
    def body(spot, blocks, out):
        pairs_body(spot, blocks, out, per_home=per_home)

    return pl.pallas_call(
        body,
        out_shape=jax.ShapeDtypeStruct((own_slots,) + blocks.shape[1:], F32),
        grid_spec=pltpu.PrefetchScalarGridSpec(
            num_scalar_prefetch=1,
            grid=(1,),
            in_specs=[pl.BlockSpec(blocks.shape, lambda i, *_: (0, 0, 0))],
            out_specs=pl.BlockSpec((own_slots,) + blocks.shape[1:], lambda i, *_: (0, 0, 0)),
        ),
        compiler_params=pltpu.CompilerParams(vmem_limit_bytes=16 << 20),
        cost_estimate=pl.CostEstimate(flops=1 << 18, bytes_accessed=3 << 20, transcendentals=0),
        name="join_pairs",
    )(spot, blocks)


def settle(held, blocks, own_most, local_slots, n, group):
    parts = blocks.shape[0]
    per = parts // local_slots

    def body(held, src, out):
        plain = held[0]
        swap = (lax.axis_index("virt") * local_slots < OFF_DIAG).astype(jnp.int32)
        first = pl.program_id(0) * group

        def as_is(g):
            for i in range(local_slots):
                out[i, g] = src[i * per : (i + 1) * per, g].reshape(n, n)

        def turned(g):
            for i in range(local_slots):
                base = jnp.where(swap != 0, local_slots - 1 - i, i) * per
                out[i, g] = src[pl.ds(base, per), g].reshape(n, n).T

        @pl.when(first + group <= plain)
        def _():
            for g in range(group):
                as_is(g)

        @pl.when(first >= plain)
        def _():
            for g in range(group):
                turned(g)

        @pl.when((first < plain) & (first + group > plain))
        def _():
            for g in range(group):
                pl.when(first + g < plain)(functools.partial(as_is, g))
                pl.when(first + g >= plain)(functools.partial(turned, g))

    return pl.pallas_call(
        body,
        out_shape=jax.ShapeDtypeStruct((local_slots, own_most, n, n), F32),
        grid_spec=pltpu.PrefetchScalarGridSpec(
            num_scalar_prefetch=1,
            grid=(own_most // group,),
            in_specs=[
                pl.BlockSpec(
                    (parts, group) + blocks.shape[2:], lambda i, *_: (0, i, 0, 0)
                )
            ],
            out_specs=pl.BlockSpec((local_slots, group, n, n), lambda i, *_: (0, i, 0, 0)),
        ),
        compiler_params=pltpu.CompilerParams(vmem_limit_bytes=16 << 20),
        cost_estimate=pl.CostEstimate(flops=1 << 18, bytes_accessed=4 << 20, transcendentals=0),
        name="settle",
    )(held, blocks)


def on_device(amplitudes, factors, integral_quadruple_table, pair_region, owner_map):
    pair_count = lax.axis_size("pair")
    virt_count = lax.axis_size("virt")
    my_pair = lax.axis_index("pair")
    my_virt = lax.axis_index("virt")
    local_slots, per_home, n, _ = amplitudes.shape
    pair_total = owner_map.shape[0]
    half = pair_total // 2
    own_most = 2 * per_home

    pieces = deal(amplitudes)
    amps = {0: pieces[0]}
    for d in sorted(range(1, virt_count), key=lambda d: -min(d, virt_count - d)):
        route = [(i, (i + d) % virt_count) for i in range(virt_count)]
        amps[d] = lax.ppermute(pieces[d], "virt", route)
    near = (1, virt_count - 1)
    pair_region, *first = lax.optimization_barrier((pair_region, *(amps[d] for d in near)))
    amps.update(zip(near, first))
    amps = [amps[d] for d in range(virt_count)]

    pair = my_pair * per_home + my_virt
    mirrored = (pair >= half).astype(jnp.int32)
    region = pair_region[pair % half]
    rows = integral_quadruple_table[region]
    o, left, right = rows[..., 0], rows[..., 1], rows[..., 2]
    partner = jnp.where(o < OFF_DIAG, o ^ 1, o)
    codes = jnp.where(
        mirrored != 0, partner * 256 + right * 16 + left, o * 256 + left * 16 + right
    )
    group = ((codes >> 8) * 16 + (codes & 15)).reshape(-1)
    place = jnp.arange(group.shape[0])
    met = (group[:, None] == group[None, :]) & (place[None, :] < place[:, None])
    codes = codes + jnp.where(jnp.any(met, axis=1), 0, FIRST).reshape(codes.shape)
    slot_total = codes.shape[0]
    touched = jnp.any(group[None, :] == jnp.arange(slot_total * 16)[:, None], axis=1)
    touched = touched.astype(jnp.int32).reshape(slot_total, 16)

    same = (owner_map[:, None] == owner_map[None, :]) & (
        jnp.arange(pair_total)[None, :] < jnp.arange(pair_total)[:, None]
    )
    spot = owner_map * own_most + jnp.sum(same.astype(jnp.int32), axis=1)

    plain = jnp.sum((owner_map[:half] == my_pair).astype(jnp.int32))
    held = plain.reshape(1)

    f_pair, f_turn = split_factors(lax.dynamic_index_in_dim(factors, region, 0, keepdims=False))
    amps, codes, touched, f_pair, f_turn, spot, held = lax.optimization_barrier(
        (amps, codes, touched, f_pair, f_turn, spot, held)
    )
    result = ladder(codes, touched, amps, f_pair, f_turn)
    sheets = result.reshape(virt_count * pair_count, -1, n)
    spread = lax.all_to_all(sheets, ("virt", "pair"), split_axis=0, concat_axis=0, tiled=True)
    joined = join_pairs(spot, spread, pair_count * own_most, per_home)
    arrived = lax.all_to_all(joined, "pair", split_axis=0, concat_axis=0, tiled=True)
    return settle(
        held,
        arrived.reshape(pair_count, own_most, -1, n),
        own_most,
        local_slots,
        n,
        8,
    )


def solution(mesh):
    return jax.shard_map(
        on_device,
        mesh=mesh,
        in_specs=(P("virt", "pair", None, None), P(), P(), P(), P()),
        out_specs=P("virt", "pair", None, None),
        check_vma=False,
    )
```

```python
import functools

import jax
import jax.numpy as jnp
from jax import lax
from jax.experimental import pallas as pl
from jax.experimental.pallas import tpu as pltpu
from jax.sharding import PartitionSpec as P

DOM = 4
OFF_DIAG = DOM * (DOM - 1)
F32 = jnp.float32
BF16 = jnp.bfloat16
FIRST = 1 << 12


def halves(x):
    high = x.astype(BF16)
    return high, (x - high.astype(F32)).astype(BF16)


def split_body(pair_region, factors, f_pair, f_turn, fac, sem, *, per_home):
    slots, n, _ = fac.shape
    pair = lax.axis_index("pair") * per_home + lax.axis_index("virt")
    region = pair_region[lax.rem(pair, pair_region.shape[0])]
    copy = pltpu.make_async_copy(factors.at[region], fac, sem)
    copy.start()
    copy.wait()
    for l in range(slots):
        tile = fac[l]
        rows = slice(l * n, (l + 1) * n)
        f_pair[rows, :n], f_pair[rows, n:] = halves(tile)
        f_turn[rows, :n], f_turn[rows, n:] = halves(tile.T)


def split_factors(pair_region, factors, per_home):
    _, slots, n, _ = factors.shape
    shape = jax.ShapeDtypeStruct((slots * n, 2 * n), BF16)
    spec = pl.BlockSpec(shape.shape, lambda i, *_: (0, 0))
    return pl.pallas_call(
        functools.partial(split_body, per_home=per_home),
        out_shape=[shape, shape],
        grid_spec=pltpu.PrefetchScalarGridSpec(
            num_scalar_prefetch=1,
            grid=(1,),
            in_specs=[pl.BlockSpec(memory_space=pltpu.HBM)],
            out_specs=[spec, spec],
            scratch_shapes=[pltpu.VMEM((slots, n, n), F32), pltpu.SemaphoreType.DMA(())],
        ),
        compiler_params=pltpu.CompilerParams(vmem_limit_bytes=16 << 20),
        cost_estimate=pl.CostEstimate(flops=1 << 20, bytes_accessed=3 << 20, transcendentals=0),
        name="split_factors",
    )(pair_region, pltpu.with_memory_space_constraint(factors, pltpu.HBM))


def deal_body(source, *refs):
    outs, sems = refs[:-1], refs[-1]
    count = len(outs)
    copies = []
    for d, out in enumerate(outs):
        to = lax.rem(lax.axis_index("virt") + d, count)
        for i in range(out.shape[0]):
            copies.append(pltpu.make_async_copy(source.at[i, to], out.at[i], sems.at[d, i]))
    for copy in copies:
        copy.start()
    for copy in copies:
        copy.wait()


def deal(amplitudes):
    local, count, n, _ = amplitudes.shape
    anywhere = pl.BlockSpec(memory_space=pl.ANY)
    return pl.pallas_call(
        deal_body,
        out_shape=[jax.ShapeDtypeStruct((local, n, n), F32)] * count,
        in_specs=[anywhere],
        out_specs=[anywhere] * count,
        scratch_shapes=[pltpu.SemaphoreType.DMA((count, local))],
        compiler_params=pltpu.CompilerParams(vmem_limit_bytes=4 << 20),
        cost_estimate=pl.CostEstimate(flops=0, bytes_accessed=2 << 20, transcendentals=0),
        name="deal",
    )(pltpu.with_memory_space_constraint(amplitudes, pltpu.HBM))


def ladder_body(
    codes, touched, *refs
):
    f_pair, f_turn, out, amp_high, amp_low, prod_a, prod_b, grouped = refs[-8:]
    amps = refs[:-8]
    slots, n, _ = out.shape
    entries = codes.shape[1]
    mirrored = (lax.axis_index("pair") >= lax.axis_size("pair") // 2).astype(jnp.int32)

    def put(v, i, tile):
        high, low = halves(tile)
        amp_high[v, :n, i * n : (i + 1) * n] = high
        amp_high[v, n:, i * n : (i + 1) * n] = high
        amp_low[v, :, i * n : (i + 1) * n] = low

    count = len(amps)
    origins = [lax.rem(lax.axis_index("virt") + (count - d), count) for d in range(count)]

    @pl.when(mirrored == 0)
    def _():
        for v, amp in zip(origins, amps):
            for i in range(amp.shape[0]):
                put(v, i, amp[i])

    @pl.when(mirrored != 0)
    def _():
        for v, amp in zip(origins, amps):
            for i in range(amp.shape[0]):
                put(v, i, amp[i].T)

    chunks = 4
    height = slots * n // chunks
    per = 2 * entries // chunks

    def product(v, prod, q):
        rows = slice(q * height, (q + 1) * height)
        prod[rows] = jnp.dot(
            f_pair[rows], amp_high[v], preferred_element_type=F32
        ) + jnp.dot(f_pair[rows, :n], amp_low[v], preferred_element_type=F32)

    def collect(v, prod, q):
        for e in range(q * per, (q + 1) * per):
            i, k = e // entries, e % entries
            code = codes[2 * v + i, k]
            to = pl.ds(pl.multiple_of(((code >> 8) & 15) * n, n), n)
            source = pl.ds(pl.multiple_of(((code >> 4) & 15) * n, n), n)
            new = prod[source, i * n : (i + 1) * n]
            r = code & 15
            grouped[r, to, :] = jnp.where(code >= FIRST, new, grouped[r, to, :] + new)

    for q in range(chunks):
        product(0, prod_a, q)

    def two(w, c):
        v = 2 * w
        for q in range(chunks):
            product(v + 1, prod_b, q)
            collect(v, prod_a, q)
        for q in range(chunks):
            product(v + 2, prod_a, q)
            collect(v + 1, prod_b, q)
        return c

    lax.fori_loop(0, slots // 4 - 1, two, 0)
    last = slots // 2 - 1
    for q in range(chunks):
        product(last, prod_b, q)
        collect(last - 1, prod_a, q)
    for q in range(chunks):
        collect(last, prod_b, q)

    step = 4
    for g in range(0, slots, step):

        def block(r):
            return jnp.concatenate(
                [
                    jnp.where(touched[o, r] > 0, grouped[r, o * n : (o + 1) * n, :], 0.0)
                    for o in range(g, g + step)
                ],
                axis=0,
            )

        parts = [halves(block(r)) for r in range(slots)]
        high = jnp.concatenate([a for a, _ in parts], axis=1)
        low = jnp.concatenate([b for _, b in parts], axis=1)
        both = jnp.dot(high, f_turn[...], preferred_element_type=F32)
        rest = jnp.dot(low, f_turn[:, :n], preferred_element_type=F32)
        total = both[:, :n] + both[:, n:] + rest
        out[g : g + step] = total.reshape(step, n, n)


def ladder(codes, touched, amps, f_pair, f_turn):
    local, n, _ = amps[0].shape
    slots = local * len(amps)
    wide = slots * n
    few = pl.BlockSpec((local, n, n), lambda i, *_: (0, 0, 0))
    whole = pl.BlockSpec((slots, n, n), lambda i, *_: (0, 0, 0))
    table = pl.BlockSpec((wide, 2 * n), lambda i, *_: (0, 0))
    return pl.pallas_call(
        ladder_body,
        out_shape=jax.ShapeDtypeStruct((slots, n, n), F32),
        grid_spec=pltpu.PrefetchScalarGridSpec(
            num_scalar_prefetch=2,
            grid=(1,),
            in_specs=[few] * len(amps) + [table, table],
            out_specs=whole,
            scratch_shapes=[
                pltpu.VMEM((slots // 2, 2 * n, 2 * n), BF16),
                pltpu.VMEM((slots // 2, n, 2 * n), BF16),
                pltpu.VMEM((wide, 2 * n), F32),
                pltpu.VMEM((wide, 2 * n), F32),
                pltpu.VMEM((slots, wide, n), F32),
            ],
        ),
        compiler_params=pltpu.CompilerParams(vmem_limit_bytes=48 << 20),
        cost_estimate=pl.CostEstimate(
            flops=12 * wide * wide * n, bytes_accessed=4 << 20, transcendentals=0
        ),
        name="ladder",
    )(codes, touched, *amps, f_pair, f_turn)


def pairs_body(spot, blocks, out, *, per_home):
    count = blocks.shape[0]
    homes = count // per_home
    half = count // 2
    out[...] = jnp.zeros(out.shape, F32)

    def home(h, c):
        for v in range(per_home):
            row = v * homes + h
            q = h * per_home + v
            value = blocks[row] + blocks[row + homes // 2]
            out[spot[q]] = value
            out[spot[q + half]] = value
        return c

    lax.fori_loop(0, homes // 2, home, 0)


def join_pairs(spot, blocks, own_slots, per_home):
    def body(spot, blocks, out):
        pairs_body(spot, blocks, out, per_home=per_home)

    return pl.pallas_call(
        body,
        out_shape=jax.ShapeDtypeStruct((own_slots,) + blocks.shape[1:], F32),
        grid_spec=pltpu.PrefetchScalarGridSpec(
            num_scalar_prefetch=1,
            grid=(1,),
            in_specs=[pl.BlockSpec(blocks.shape, lambda i, *_: (0, 0, 0))],
            out_specs=pl.BlockSpec((own_slots,) + blocks.shape[1:], lambda i, *_: (0, 0, 0)),
        ),
        compiler_params=pltpu.CompilerParams(vmem_limit_bytes=16 << 20),
        cost_estimate=pl.CostEstimate(flops=1 << 18, bytes_accessed=3 << 20, transcendentals=0),
        name="join_pairs",
    )(spot, blocks)


def settle(held, blocks, own_most, local_slots, n, group):
    parts = blocks.shape[0]
    per = parts // local_slots

    def body(held, src, out):
        plain = held[0]
        swap = (lax.axis_index("virt") * local_slots < OFF_DIAG).astype(jnp.int32)
        first = pl.program_id(0) * group

        def as_is(g):
            for i in range(local_slots):
                out[i, g] = src[i * per : (i + 1) * per, g].reshape(n, n)

        def turned(g):
            for i in range(local_slots):
                base = jnp.where(swap != 0, local_slots - 1 - i, i) * per
                out[i, g] = src[pl.ds(base, per), g].reshape(n, n).T

        @pl.when(first + group <= plain)
        def _():
            for g in range(group):
                as_is(g)

        @pl.when(first >= plain)
        def _():
            for g in range(group):
                turned(g)

        @pl.when((first < plain) & (first + group > plain))
        def _():
            for g in range(group):
                pl.when(first + g < plain)(functools.partial(as_is, g))
                pl.when(first + g >= plain)(functools.partial(turned, g))

    return pl.pallas_call(
        body,
        out_shape=jax.ShapeDtypeStruct((local_slots, own_most, n, n), F32),
        grid_spec=pltpu.PrefetchScalarGridSpec(
            num_scalar_prefetch=1,
            grid=(own_most // group,),
            in_specs=[
                pl.BlockSpec(
                    (parts, group) + blocks.shape[2:], lambda i, *_: (0, i, 0, 0)
                )
            ],
            out_specs=pl.BlockSpec((local_slots, group, n, n), lambda i, *_: (0, i, 0, 0)),
        ),
        compiler_params=pltpu.CompilerParams(vmem_limit_bytes=16 << 20),
        cost_estimate=pl.CostEstimate(flops=1 << 18, bytes_accessed=4 << 20, transcendentals=0),
        name="settle",
    )(held, blocks)


def on_device(amplitudes, factors, integral_quadruple_table, pair_region, owner_map):
    pair_count = lax.axis_size("pair")
    virt_count = lax.axis_size("virt")
    my_pair = lax.axis_index("pair")
    my_virt = lax.axis_index("virt")
    local_slots, per_home, n, _ = amplitudes.shape
    pair_total = owner_map.shape[0]
    half = pair_total // 2
    own_most = 2 * per_home

    pieces = deal(amplitudes)
    amps = {0: pieces[0]}
    for d in sorted(range(1, virt_count), key=lambda d: -min(d, virt_count - d)):
        route = [(i, (i + d) % virt_count) for i in range(virt_count)]
        amps[d] = lax.ppermute(pieces[d], "virt", route)
    near = (1, virt_count - 1)
    pair_region, *first = lax.optimization_barrier((pair_region, *(amps[d] for d in near)))
    amps.update(zip(near, first))
    amps = [amps[d] for d in range(virt_count)]

    pair = my_pair * per_home + my_virt
    mirrored = (pair >= half).astype(jnp.int32)
    mine = jnp.arange(half) == lax.rem(pair, half)
    region = jnp.sum(jnp.where(mine, pair_region, 0))
    here = jnp.arange(integral_quadruple_table.shape[0]) == region
    rows = jnp.sum(jnp.where(here[:, None, None, None], integral_quadruple_table, 0), axis=0)
    o, left, right = rows[..., 0], rows[..., 1], rows[..., 2]
    partner = jnp.where(o < OFF_DIAG, o ^ 1, o)
    codes = jnp.where(
        mirrored != 0, partner * 256 + right * 16 + left, o * 256 + left * 16 + right
    )
    group = ((codes >> 8) * 16 + (codes & 15)).reshape(-1)
    place = jnp.arange(group.shape[0])
    met = (group[:, None] == group[None, :]) & (place[None, :] < place[:, None])
    codes = codes + jnp.where(jnp.any(met, axis=1), 0, FIRST).reshape(codes.shape)
    slot_total = codes.shape[0]
    touched = jnp.any(group[None, :] == jnp.arange(slot_total * 16)[:, None], axis=1)
    touched = touched.astype(jnp.int32).reshape(slot_total, 16)

    same = (owner_map[:, None] == owner_map[None, :]) & (
        jnp.arange(pair_total)[None, :] < jnp.arange(pair_total)[:, None]
    )
    spot = owner_map * own_most + jnp.sum(same.astype(jnp.int32), axis=1)

    plain = jnp.sum((owner_map[:half] == my_pair).astype(jnp.int32))
    held = plain.reshape(1)

    f_pair, f_turn = split_factors(pair_region, factors, per_home)
    amps, codes, touched, f_pair, f_turn, spot, held = lax.optimization_barrier(
        (amps, codes, touched, f_pair, f_turn, spot, held)
    )
    result = ladder(codes, touched, amps, f_pair, f_turn)
    sheets = result.reshape(virt_count * pair_count, -1, n)
    spread = lax.all_to_all(sheets, ("virt", "pair"), split_axis=0, concat_axis=0, tiled=True)
    joined = join_pairs(spot, spread, pair_count * own_most, per_home)
    arrived = lax.all_to_all(joined, "pair", split_axis=0, concat_axis=0, tiled=True)
    return settle(
        held,
        arrived.reshape(pair_count, own_most, -1, n),
        own_most,
        local_slots,
        n,
        8,
    )


def solution(mesh):
    return jax.shard_map(
        on_device,
        mesh=mesh,
        in_specs=(P("virt", "pair", None, None), P(), P(), P(), P()),
        out_specs=P("virt", "pair", None, None),
        check_vma=False,
    )
```

```python
import functools

import jax
import jax.numpy as jnp
from jax import lax
from jax.experimental import pallas as pl
from jax.experimental.pallas import tpu as pltpu
from jax.sharding import PartitionSpec as P

DOM = 4
OFF_DIAG = DOM * (DOM - 1)
F32 = jnp.float32
BF16 = jnp.bfloat16
FIRST = 1 << 12


def halves(x):
    high = x.astype(BF16)
    return high, (x - high.astype(F32)).astype(BF16)


def split_body(pair_region, factors, f_pair, f_turn, fac, sem, *, per_home):
    slots, n, _ = fac.shape
    pair = lax.axis_index("pair") * per_home + lax.axis_index("virt")
    region = pair_region[lax.rem(pair, pair_region.shape[0])]
    copy = pltpu.make_async_copy(factors.at[region], fac, sem)
    copy.start()
    copy.wait()
    for l in range(slots):
        tile = fac[l]
        rows = slice(l * n, (l + 1) * n)
        f_pair[rows, :n], f_pair[rows, n:] = halves(tile)
        f_turn[rows, :n], f_turn[rows, n:] = halves(tile.T)


def split_factors(pair_region, factors, per_home):
    _, slots, n, _ = factors.shape
    shape = jax.ShapeDtypeStruct((slots * n, 2 * n), BF16)
    spec = pl.BlockSpec(shape.shape, lambda i, *_: (0, 0))
    return pl.pallas_call(
        functools.partial(split_body, per_home=per_home),
        out_shape=[shape, shape],
        grid_spec=pltpu.PrefetchScalarGridSpec(
            num_scalar_prefetch=1,
            grid=(1,),
            in_specs=[pl.BlockSpec(memory_space=pltpu.HBM)],
            out_specs=[spec, spec],
            scratch_shapes=[pltpu.VMEM((slots, n, n), F32), pltpu.SemaphoreType.DMA(())],
        ),
        compiler_params=pltpu.CompilerParams(vmem_limit_bytes=16 << 20),
        cost_estimate=pl.CostEstimate(flops=1 << 20, bytes_accessed=3 << 20, transcendentals=0),
        name="split_factors",
    )(pair_region, pltpu.with_memory_space_constraint(factors, pltpu.HBM))


def deal_body(source, pair_region, owner_map, *refs):
    *outs, regions, owners, sems, small = refs
    count = len(outs)
    copies = []
    for d, out in enumerate(outs):
        to = lax.rem(lax.axis_index("virt") + d, count)
        for i in range(out.shape[0]):
            copies.append(pltpu.make_async_copy(source.at[i, to], out.at[i], sems.at[d, i]))
    copies.append(pltpu.make_async_copy(pair_region, regions, small.at[0]))
    copies.append(pltpu.make_async_copy(owner_map, owners, small.at[1]))
    for copy in copies:
        copy.start()
    for copy in copies:
        copy.wait()


def deal(amplitudes, pair_region, owner_map):
    local, count, n, _ = amplitudes.shape
    anywhere = pl.BlockSpec(memory_space=pl.ANY)
    *pieces, regions, owners = pl.pallas_call(
        deal_body,
        out_shape=[jax.ShapeDtypeStruct((local, n, n), F32)] * count
        + [jax.ShapeDtypeStruct(x.shape, x.dtype) for x in (pair_region, owner_map)],
        in_specs=[anywhere] * 3,
        out_specs=[anywhere] * (count + 2),
        scratch_shapes=[pltpu.SemaphoreType.DMA((count, local)), pltpu.SemaphoreType.DMA((2,))],
        compiler_params=pltpu.CompilerParams(vmem_limit_bytes=4 << 20),
        cost_estimate=pl.CostEstimate(flops=0, bytes_accessed=2 << 20, transcendentals=0),
        name="deal",
    )(*(pltpu.with_memory_space_constraint(x, pltpu.HBM) for x in (amplitudes, pair_region, owner_map)))
    return pieces, regions, owners


def ladder_body(
    codes, touched, *refs
):
    f_pair, f_turn, out, amp_high, amp_low, prod_a, prod_b, grouped = refs[-8:]
    amps = refs[:-8]
    slots, n, _ = out.shape
    entries = codes.shape[1]
    mirrored = (lax.axis_index("pair") >= lax.axis_size("pair") // 2).astype(jnp.int32)

    def put(v, i, tile):
        high, low = halves(tile)
        amp_high[v, :n, i * n : (i + 1) * n] = high
        amp_high[v, n:, i * n : (i + 1) * n] = high
        amp_low[v, :, i * n : (i + 1) * n] = low

    count = len(amps)
    origins = [lax.rem(lax.axis_index("virt") + (count - d), count) for d in range(count)]

    @pl.when(mirrored == 0)
    def _():
        for v, amp in zip(origins, amps):
            for i in range(amp.shape[0]):
                put(v, i, amp[i])

    @pl.when(mirrored != 0)
    def _():
        for v, amp in zip(origins, amps):
            for i in range(amp.shape[0]):
                put(v, i, amp[i].T)

    chunks = 4
    height = slots * n // chunks
    per = 2 * entries // chunks

    def product(v, prod, q):
        rows = slice(q * height, (q + 1) * height)
        prod[rows] = jnp.dot(
            f_pair[rows], amp_high[v], preferred_element_type=F32
        ) + jnp.dot(f_pair[rows, :n], amp_low[v], preferred_element_type=F32)

    def collect(v, prod, q):
        for e in range(q * per, (q + 1) * per):
            i, k = e // entries, e % entries
            code = codes[2 * v + i, k]
            to = pl.ds(pl.multiple_of(((code >> 8) & 15) * n, n), n)
            source = pl.ds(pl.multiple_of(((code >> 4) & 15) * n, n), n)
            new = prod[source, i * n : (i + 1) * n]
            r = code & 15
            grouped[r, to, :] = jnp.where(code >= FIRST, new, grouped[r, to, :] + new)

    for q in range(chunks):
        product(0, prod_a, q)

    def two(w, c):
        v = 2 * w
        for q in range(chunks):
            product(v + 1, prod_b, q)
            collect(v, prod_a, q)
        for q in range(chunks):
            product(v + 2, prod_a, q)
            collect(v + 1, prod_b, q)
        return c

    lax.fori_loop(0, slots // 4 - 1, two, 0)
    last = slots // 2 - 1
    for q in range(chunks):
        product(last, prod_b, q)
        collect(last - 1, prod_a, q)
    for q in range(chunks):
        collect(last, prod_b, q)

    step = 4
    for g in range(0, slots, step):

        def block(r):
            return jnp.concatenate(
                [
                    jnp.where(touched[o, r] > 0, grouped[r, o * n : (o + 1) * n, :], 0.0)
                    for o in range(g, g + step)
                ],
                axis=0,
            )

        parts = [halves(block(r)) for r in range(slots)]
        high = jnp.concatenate([a for a, _ in parts], axis=1)
        low = jnp.concatenate([b for _, b in parts], axis=1)
        both = jnp.dot(high, f_turn[...], preferred_element_type=F32)
        rest = jnp.dot(low, f_turn[:, :n], preferred_element_type=F32)
        total = both[:, :n] + both[:, n:] + rest
        out[g : g + step] = total.reshape(step, n, n)


def ladder(codes, touched, amps, f_pair, f_turn):
    local, n, _ = amps[0].shape
    slots = local * len(amps)
    wide = slots * n
    few = pl.BlockSpec((local, n, n), lambda i, *_: (0, 0, 0))
    whole = pl.BlockSpec((slots, n, n), lambda i, *_: (0, 0, 0))
    table = pl.BlockSpec((wide, 2 * n), lambda i, *_: (0, 0))
    return pl.pallas_call(
        ladder_body,
        out_shape=jax.ShapeDtypeStruct((slots, n, n), F32),
        grid_spec=pltpu.PrefetchScalarGridSpec(
            num_scalar_prefetch=2,
            grid=(1,),
            in_specs=[few] * len(amps) + [table, table],
            out_specs=whole,
            scratch_shapes=[
                pltpu.VMEM((slots // 2, 2 * n, 2 * n), BF16),
                pltpu.VMEM((slots // 2, n, 2 * n), BF16),
                pltpu.VMEM((wide, 2 * n), F32),
                pltpu.VMEM((wide, 2 * n), F32),
                pltpu.VMEM((slots, wide, n), F32),
            ],
        ),
        compiler_params=pltpu.CompilerParams(vmem_limit_bytes=48 << 20),
        cost_estimate=pl.CostEstimate(
            flops=12 * wide * wide * n, bytes_accessed=4 << 20, transcendentals=0
        ),
        name="ladder",
    )(codes, touched, *amps, f_pair, f_turn)


def pairs_body(spot, blocks, out, *, per_home):
    count = blocks.shape[0]
    homes = count // per_home
    half = count // 2
    out[...] = jnp.zeros(out.shape, F32)

    def home(h, c):
        for v in range(per_home):
            row = v * homes + h
            q = h * per_home + v
            value = blocks[row] + blocks[row + homes // 2]
            out[spot[q]] = value
            out[spot[q + half]] = value
        return c

    lax.fori_loop(0, homes // 2, home, 0)


def join_pairs(spot, blocks, own_slots, per_home):
    def body(spot, blocks, out):
        pairs_body(spot, blocks, out, per_home=per_home)

    return pl.pallas_call(
        body,
        out_shape=jax.ShapeDtypeStruct((own_slots,) + blocks.shape[1:], F32),
        grid_spec=pltpu.PrefetchScalarGridSpec(
            num_scalar_prefetch=1,
            grid=(1,),
            in_specs=[pl.BlockSpec(blocks.shape, lambda i, *_: (0, 0, 0))],
            out_specs=pl.BlockSpec((own_slots,) + blocks.shape[1:], lambda i, *_: (0, 0, 0)),
        ),
        compiler_params=pltpu.CompilerParams(vmem_limit_bytes=16 << 20),
        cost_estimate=pl.CostEstimate(flops=1 << 18, bytes_accessed=3 << 20, transcendentals=0),
        name="join_pairs",
    )(spot, blocks)


def settle(held, blocks, own_most, local_slots, n, group):
    parts = blocks.shape[0]
    per = parts // local_slots

    def body(held, src, out):
        plain = held[0]
        swap = (lax.axis_index("virt") * local_slots < OFF_DIAG).astype(jnp.int32)
        first = pl.program_id(0) * group

        def as_is(g):
            for i in range(local_slots):
                out[i, g] = src[i * per : (i + 1) * per, g].reshape(n, n)

        def turned(g):
            for i in range(local_slots):
                base = jnp.where(swap != 0, local_slots - 1 - i, i) * per
                out[i, g] = src[pl.ds(base, per), g].reshape(n, n).T

        @pl.when(first + group <= plain)
        def _():
            for g in range(group):
                as_is(g)

        @pl.when(first >= plain)
        def _():
            for g in range(group):
                turned(g)

        @pl.when((first < plain) & (first + group > plain))
        def _():
            for g in range(group):
                pl.when(first + g < plain)(functools.partial(as_is, g))
                pl.when(first + g >= plain)(functools.partial(turned, g))

    return pl.pallas_call(
        body,
        out_shape=jax.ShapeDtypeStruct((local_slots, own_most, n, n), F32),
        grid_spec=pltpu.PrefetchScalarGridSpec(
            num_scalar_prefetch=1,
            grid=(own_most // group,),
            in_specs=[
                pl.BlockSpec(
                    (parts, group) + blocks.shape[2:], lambda i, *_: (0, i, 0, 0)
                )
            ],
            out_specs=pl.BlockSpec((local_slots, group, n, n), lambda i, *_: (0, i, 0, 0)),
        ),
        compiler_params=pltpu.CompilerParams(vmem_limit_bytes=16 << 20),
        cost_estimate=pl.CostEstimate(flops=1 << 18, bytes_accessed=4 << 20, transcendentals=0),
        name="settle",
    )(held, blocks)


def on_device(amplitudes, factors, integral_quadruple_table, pair_region, owner_map):
    pair_count = lax.axis_size("pair")
    virt_count = lax.axis_size("virt")
    my_pair = lax.axis_index("pair")
    my_virt = lax.axis_index("virt")
    local_slots, per_home, n, _ = amplitudes.shape
    pair_total = owner_map.shape[0]
    half = pair_total // 2
    own_most = 2 * per_home

    pieces, pair_region, owner_map = deal(amplitudes, pair_region, owner_map)
    amps = {0: pieces[0]}
    for d in sorted(range(1, virt_count), key=lambda d: -min(d, virt_count - d)):
        route = [(i, (i + d) % virt_count) for i in range(virt_count)]
        amps[d] = lax.ppermute(pieces[d], "virt", route)
    near = (1, virt_count - 1)
    pair_region, owner_map, *first = lax.optimization_barrier(
        (pair_region, owner_map, *(amps[d] for d in near))
    )
    amps.update(zip(near, first))
    amps = [amps[d] for d in range(virt_count)]

    pair = my_pair * per_home + my_virt
    mirrored = (pair >= half).astype(jnp.int32)
    mine = jnp.arange(half) == lax.rem(pair, half)
    region = jnp.sum(jnp.where(mine, pair_region, 0))
    here = jnp.arange(integral_quadruple_table.shape[0]) == region
    rows = jnp.sum(jnp.where(here[:, None, None, None], integral_quadruple_table, 0), axis=0)
    o, left, right = rows[..., 0], rows[..., 1], rows[..., 2]
    partner = jnp.where(o < OFF_DIAG, o ^ 1, o)
    codes = jnp.where(
        mirrored != 0, partner * 256 + right * 16 + left, o * 256 + left * 16 + right
    )
    group = ((codes >> 8) * 16 + (codes & 15)).reshape(-1)
    place = jnp.arange(group.shape[0])
    met = (group[:, None] == group[None, :]) & (place[None, :] < place[:, None])
    codes = codes + jnp.where(jnp.any(met, axis=1), 0, FIRST).reshape(codes.shape)
    slot_total = codes.shape[0]
    touched = jnp.any(group[None, :] == jnp.arange(slot_total * 16)[:, None], axis=1)
    touched = touched.astype(jnp.int32).reshape(slot_total, 16)

    same = (owner_map[:, None] == owner_map[None, :]) & (
        jnp.arange(pair_total)[None, :] < jnp.arange(pair_total)[:, None]
    )
    spot = owner_map * own_most + jnp.sum(same.astype(jnp.int32), axis=1)

    plain = jnp.sum((owner_map[:half] == my_pair).astype(jnp.int32))
    held = plain.reshape(1)

    f_pair, f_turn = split_factors(pair_region, factors, per_home)
    amps, codes, touched, f_pair, f_turn, spot, held = lax.optimization_barrier(
        (amps, codes, touched, f_pair, f_turn, spot, held)
    )
    result = ladder(codes, touched, amps, f_pair, f_turn)
    sheets = result.reshape(virt_count * pair_count, -1, n)
    spread = lax.all_to_all(sheets, ("virt", "pair"), split_axis=0, concat_axis=0, tiled=True)
    joined = join_pairs(spot, spread, pair_count * own_most, per_home)
    arrived = lax.all_to_all(joined, "pair", split_axis=0, concat_axis=0, tiled=True)
    return settle(
        held,
        arrived.reshape(pair_count, own_most, -1, n),
        own_most,
        local_slots,
        n,
        8,
    )


def solution(mesh):
    return jax.shard_map(
        on_device,
        mesh=mesh,
        in_specs=(P("virt", "pair", None, None), P(), P(), P(), P()),
        out_specs=P("virt", "pair", None, None),
        check_vma=False,
    )
```

```python
import functools

import jax
import jax.numpy as jnp
from jax import lax
from jax.experimental import pallas as pl
from jax.experimental.pallas import tpu as pltpu
from jax.sharding import PartitionSpec as P

DOM = 4
OFF_DIAG = DOM * (DOM - 1)
F32 = jnp.float32
BF16 = jnp.bfloat16
FIRST = 1 << 12


def halves(x):
    high = x.astype(BF16)
    return high, (x - high.astype(F32)).astype(BF16)


def split_body(pair_region, factors, f_pair, f_turn, fac, sem, *, per_home):
    slots, n, _ = fac.shape
    pair = lax.axis_index("pair") * per_home + lax.axis_index("virt")
    region = pair_region[lax.rem(pair, pair_region.shape[0])]
    copy = pltpu.make_async_copy(factors.at[region], fac, sem)
    copy.start()
    copy.wait()
    for l in range(slots):
        tile = fac[l]
        rows = slice(l * n, (l + 1) * n)
        f_pair[rows, :n], f_pair[rows, n:] = halves(tile)
        f_turn[rows, :n], f_turn[rows, n:] = halves(tile.T)


def split_factors(pair_region, factors, per_home):
    _, slots, n, _ = factors.shape
    shape = jax.ShapeDtypeStruct((slots * n, 2 * n), BF16)
    spec = pl.BlockSpec(shape.shape, lambda i, *_: (0, 0))
    return pl.pallas_call(
        functools.partial(split_body, per_home=per_home),
        out_shape=[shape, shape],
        grid_spec=pltpu.PrefetchScalarGridSpec(
            num_scalar_prefetch=1,
            grid=(1,),
            in_specs=[pl.BlockSpec(memory_space=pltpu.HBM)],
            out_specs=[spec, spec],
            scratch_shapes=[pltpu.VMEM((slots, n, n), F32), pltpu.SemaphoreType.DMA(())],
        ),
        compiler_params=pltpu.CompilerParams(vmem_limit_bytes=16 << 20),
        cost_estimate=pl.CostEstimate(flops=1 << 20, bytes_accessed=3 << 20, transcendentals=0),
        name="split_factors",
    )(pair_region, pltpu.with_memory_space_constraint(factors, pltpu.HBM))


def deal_body(source, pair_region, owner_map, *refs):
    *outs, regions, owners, sems, small = refs
    count = len(outs)
    copies = []
    for d, out in enumerate(outs):
        to = lax.rem(lax.axis_index("virt") + d, count)
        for i in range(out.shape[0]):
            copies.append(pltpu.make_async_copy(source.at[i, to], out.at[i], sems.at[d, i]))
    copies.append(pltpu.make_async_copy(pair_region, regions, small.at[0]))
    copies.append(pltpu.make_async_copy(owner_map, owners, small.at[1]))
    for copy in copies:
        copy.start()
    for copy in copies:
        copy.wait()


def deal(amplitudes, pair_region, owner_map):
    local, count, n, _ = amplitudes.shape
    anywhere = pl.BlockSpec(memory_space=pl.ANY)
    *pieces, regions, owners = pl.pallas_call(
        deal_body,
        out_shape=[jax.ShapeDtypeStruct((local, n, n), F32)] * count
        + [jax.ShapeDtypeStruct(x.shape, x.dtype) for x in (pair_region, owner_map)],
        in_specs=[anywhere] * 3,
        out_specs=[anywhere] * (count + 2),
        scratch_shapes=[pltpu.SemaphoreType.DMA((count, local)), pltpu.SemaphoreType.DMA((2,))],
        compiler_params=pltpu.CompilerParams(vmem_limit_bytes=4 << 20),
        cost_estimate=pl.CostEstimate(flops=0, bytes_accessed=2 << 20, transcendentals=0),
        name="deal",
    )(*(pltpu.with_memory_space_constraint(x, pltpu.HBM) for x in (amplitudes, pair_region, owner_map)))
    return pieces, regions, owners


def ladder_body(
    codes, touched, *refs, steps
):
    f_pair, f_turn, out, amp_high, amp_low, prod_a, prod_b, grouped = refs[-8:]
    amps = refs[:-8]
    slots, n, _ = out.shape
    entries = codes.shape[1]
    mirrored = (lax.axis_index("pair") >= lax.axis_size("pair") // 2).astype(jnp.int32)

    def put(v, i, tile):
        high, low = halves(tile)
        amp_high[v, :n, i * n : (i + 1) * n] = high
        amp_high[v, n:, i * n : (i + 1) * n] = high
        amp_low[v, :, i * n : (i + 1) * n] = low

    count = len(amps)
    origins = [lax.rem(lax.axis_index("virt") + (count - d), count) for d in steps]

    @pl.when(mirrored == 0)
    def _():
        for v, amp in zip(origins, amps):
            for i in range(amp.shape[0]):
                put(v, i, amp[i])

    @pl.when(mirrored != 0)
    def _():
        for v, amp in zip(origins, amps):
            for i in range(amp.shape[0]):
                put(v, i, amp[i].T)

    chunks = 4
    height = slots * n // chunks
    per = 2 * entries // chunks

    def product(v, prod, q):
        rows = slice(q * height, (q + 1) * height)
        prod[rows] = jnp.dot(
            f_pair[rows], amp_high[v], preferred_element_type=F32
        ) + jnp.dot(f_pair[rows, :n], amp_low[v], preferred_element_type=F32)

    def collect(v, prod, q):
        for e in range(q * per, (q + 1) * per):
            i, k = e // entries, e % entries
            code = codes[2 * v + i, k]
            to = pl.ds(pl.multiple_of(((code >> 8) & 15) * n, n), n)
            source = pl.ds(pl.multiple_of(((code >> 4) & 15) * n, n), n)
            new = prod[source, i * n : (i + 1) * n]
            r = code & 15
            grouped[r, to, :] = jnp.where(code >= FIRST, new, grouped[r, to, :] + new)

    for q in range(chunks):
        product(0, prod_a, q)

    def two(w, c):
        v = 2 * w
        for q in range(chunks):
            product(v + 1, prod_b, q)
            collect(v, prod_a, q)
        for q in range(chunks):
            product(v + 2, prod_a, q)
            collect(v + 1, prod_b, q)
        return c

    lax.fori_loop(0, slots // 4 - 1, two, 0)
    last = slots // 2 - 1
    for q in range(chunks):
        product(last, prod_b, q)
        collect(last - 1, prod_a, q)
    for q in range(chunks):
        collect(last, prod_b, q)

    step = 4
    for g in range(0, slots, step):

        def block(r):
            return jnp.concatenate(
                [
                    jnp.where(touched[o, r] > 0, grouped[r, o * n : (o + 1) * n, :], 0.0)
                    for o in range(g, g + step)
                ],
                axis=0,
            )

        parts = [halves(block(r)) for r in range(slots)]
        high = jnp.concatenate([a for a, _ in parts], axis=1)
        low = jnp.concatenate([b for _, b in parts], axis=1)
        both = jnp.dot(high, f_turn[...], preferred_element_type=F32)
        rest = jnp.dot(low, f_turn[:, :n], preferred_element_type=F32)
        total = both[:, :n] + both[:, n:] + rest
        out[g : g + step] = total.reshape(step, n, n)


def ladder(codes, touched, amps, steps, f_pair, f_turn):
    local, n, _ = amps[0].shape
    slots = local * len(amps)
    wide = slots * n
    few = pl.BlockSpec((local, n, n), lambda i, *_: (0, 0, 0))
    whole = pl.BlockSpec((slots, n, n), lambda i, *_: (0, 0, 0))
    table = pl.BlockSpec((wide, 2 * n), lambda i, *_: (0, 0))
    return pl.pallas_call(
        functools.partial(ladder_body, steps=steps),
        out_shape=jax.ShapeDtypeStruct((slots, n, n), F32),
        grid_spec=pltpu.PrefetchScalarGridSpec(
            num_scalar_prefetch=2,
            grid=(1,),
            in_specs=[few] * len(amps) + [table, table],
            out_specs=whole,
            scratch_shapes=[
                pltpu.VMEM((slots // 2, 2 * n, 2 * n), BF16),
                pltpu.VMEM((slots // 2, n, 2 * n), BF16),
                pltpu.VMEM((wide, 2 * n), F32),
                pltpu.VMEM((wide, 2 * n), F32),
                pltpu.VMEM((slots, wide, n), F32),
            ],
        ),
        compiler_params=pltpu.CompilerParams(vmem_limit_bytes=48 << 20),
        cost_estimate=pl.CostEstimate(
            flops=12 * wide * wide * n, bytes_accessed=4 << 20, transcendentals=0
        ),
        name="ladder",
    )(codes, touched, *amps, f_pair, f_turn)


def pairs_body(spot, blocks, out, *, per_home):
    count = blocks.shape[0]
    homes = count // per_home
    half = count // 2
    out[...] = jnp.zeros(out.shape, F32)

    def home(h, c):
        for v in range(per_home):
            row = v * homes + h
            q = h * per_home + v
            value = blocks[row] + blocks[row + homes // 2]
            out[spot[q]] = value
            out[spot[q + half]] = value
        return c

    lax.fori_loop(0, homes // 2, home, 0)


def join_pairs(spot, blocks, own_slots, per_home):
    def body(spot, blocks, out):
        pairs_body(spot, blocks, out, per_home=per_home)

    return pl.pallas_call(
        body,
        out_shape=jax.ShapeDtypeStruct((own_slots,) + blocks.shape[1:], F32),
        grid_spec=pltpu.PrefetchScalarGridSpec(
            num_scalar_prefetch=1,
            grid=(1,),
            in_specs=[pl.BlockSpec(blocks.shape, lambda i, *_: (0, 0, 0))],
            out_specs=pl.BlockSpec((own_slots,) + blocks.shape[1:], lambda i, *_: (0, 0, 0)),
        ),
        compiler_params=pltpu.CompilerParams(vmem_limit_bytes=16 << 20),
        cost_estimate=pl.CostEstimate(flops=1 << 18, bytes_accessed=3 << 20, transcendentals=0),
        name="join_pairs",
    )(spot, blocks)


def settle(held, blocks, own_most, local_slots, n, group):
    parts = blocks.shape[0]
    per = parts // local_slots

    def body(held, src, out):
        plain = held[0]
        swap = (lax.axis_index("virt") * local_slots < OFF_DIAG).astype(jnp.int32)
        first = pl.program_id(0) * group

        def as_is(g):
            for i in range(local_slots):
                out[i, g] = src[i * per : (i + 1) * per, g].reshape(n, n)

        def turned(g):
            for i in range(local_slots):
                base = jnp.where(swap != 0, local_slots - 1 - i, i) * per
                out[i, g] = src[pl.ds(base, per), g].reshape(n, n).T

        @pl.when(first + group <= plain)
        def _():
            for g in range(group):
                as_is(g)

        @pl.when(first >= plain)
        def _():
            for g in range(group):
                turned(g)

        @pl.when((first < plain) & (first + group > plain))
        def _():
            for g in range(group):
                pl.when(first + g < plain)(functools.partial(as_is, g))
                pl.when(first + g >= plain)(functools.partial(turned, g))

    return pl.pallas_call(
        body,
        out_shape=jax.ShapeDtypeStruct((local_slots, own_most, n, n), F32),
        grid_spec=pltpu.PrefetchScalarGridSpec(
            num_scalar_prefetch=1,
            grid=(own_most // group,),
            in_specs=[
                pl.BlockSpec(
                    (parts, group) + blocks.shape[2:], lambda i, *_: (0, i, 0, 0)
                )
            ],
            out_specs=pl.BlockSpec((local_slots, group, n, n), lambda i, *_: (0, i, 0, 0)),
        ),
        compiler_params=pltpu.CompilerParams(vmem_limit_bytes=16 << 20),
        cost_estimate=pl.CostEstimate(flops=1 << 18, bytes_accessed=4 << 20, transcendentals=0),
        name="settle",
    )(held, blocks)


def on_device(amplitudes, factors, integral_quadruple_table, pair_region, owner_map):
    pair_count = lax.axis_size("pair")
    virt_count = lax.axis_size("virt")
    my_pair = lax.axis_index("pair")
    my_virt = lax.axis_index("virt")
    local_slots, per_home, n, _ = amplitudes.shape
    pair_total = owner_map.shape[0]
    half = pair_total // 2
    own_most = 2 * per_home

    pieces, pair_region, owner_map = deal(amplitudes, pair_region, owner_map)
    amps = {0: pieces[0]}
    for d in sorted(range(1, virt_count), key=lambda d: -min(d, virt_count - d)):
        route = [(i, (i + d) % virt_count) for i in range(virt_count)]
        amps[d] = lax.ppermute(pieces[d], "virt", route)
    near = (1, virt_count - 1)
    pair_region, owner_map, *first = lax.optimization_barrier(
        (pair_region, owner_map, *(amps[d] for d in near))
    )
    amps.update(zip(near, first))
    steps = (0, *near, *sorted(set(range(1, virt_count)) - set(near), key=lambda d: -min(d, virt_count - d)))
    amps = [amps[d] for d in steps]

    pair = my_pair * per_home + my_virt
    mirrored = (pair >= half).astype(jnp.int32)
    mine = jnp.arange(half) == lax.rem(pair, half)
    region = jnp.sum(jnp.where(mine, pair_region, 0))
    here = jnp.arange(integral_quadruple_table.shape[0]) == region
    rows = jnp.sum(jnp.where(here[:, None, None, None], integral_quadruple_table, 0), axis=0)
    o, left, right = rows[..., 0], rows[..., 1], rows[..., 2]
    partner = jnp.where(o < OFF_DIAG, o ^ 1, o)
    codes = jnp.where(
        mirrored != 0, partner * 256 + right * 16 + left, o * 256 + left * 16 + right
    )
    group = ((codes >> 8) * 16 + (codes & 15)).reshape(-1)
    place = jnp.arange(group.shape[0])
    met = (group[:, None] == group[None, :]) & (place[None, :] < place[:, None])
    codes = codes + jnp.where(jnp.any(met, axis=1), 0, FIRST).reshape(codes.shape)
    slot_total = codes.shape[0]
    touched = jnp.any(group[None, :] == jnp.arange(slot_total * 16)[:, None], axis=1)
    touched = touched.astype(jnp.int32).reshape(slot_total, 16)

    same = (owner_map[:, None] == owner_map[None, :]) & (
        jnp.arange(pair_total)[None, :] < jnp.arange(pair_total)[:, None]
    )
    spot = owner_map * own_most + jnp.sum(same.astype(jnp.int32), axis=1)

    plain = jnp.sum((owner_map[:half] == my_pair).astype(jnp.int32))
    held = plain.reshape(1)

    f_pair, f_turn = split_factors(pair_region, factors, per_home)
    amps, codes, touched, f_pair, f_turn, spot, held = lax.optimization_barrier(
        (amps, codes, touched, f_pair, f_turn, spot, held)
    )
    result = ladder(codes, touched, amps, steps, f_pair, f_turn)
    sheets = result.reshape(virt_count * pair_count, -1, n)
    spread = lax.all_to_all(sheets, ("virt", "pair"), split_axis=0, concat_axis=0, tiled=True)
    joined = join_pairs(spot, spread, pair_count * own_most, per_home)
    arrived = lax.all_to_all(joined, "pair", split_axis=0, concat_axis=0, tiled=True)
    return settle(
        held,
        arrived.reshape(pair_count, own_most, -1, n),
        own_most,
        local_slots,
        n,
        8,
    )


def solution(mesh):
    return jax.shard_map(
        on_device,
        mesh=mesh,
        in_specs=(P("virt", "pair", None, None), P(), P(), P(), P()),
        out_specs=P("virt", "pair", None, None),
        check_vma=False,
    )
```

```python
import functools

import jax
import jax.numpy as jnp
from jax import lax
from jax.experimental import pallas as pl
from jax.experimental.pallas import tpu as pltpu
from jax.sharding import PartitionSpec as P

DOM = 4
OFF_DIAG = DOM * (DOM - 1)
F32 = jnp.float32
BF16 = jnp.bfloat16
FIRST = 1 << 12


def halves(x):
    high = x.astype(BF16)
    return high, (x - high.astype(F32)).astype(BF16)


def split_body(pair_region, factors, f_pair, f_turn, fac, sems, *, per_home):
    slots, n, _ = fac.shape
    pair = lax.axis_index("pair") * per_home + lax.axis_index("virt")
    region = pair_region[lax.rem(pair, pair_region.shape[0])]
    parts = sems.shape[0]
    few = slots // parts
    copies = []
    for q in range(parts):
        tiles = pl.ds(q * few, few)
        copy = pltpu.make_async_copy(factors.at[region, tiles], fac.at[tiles], sems.at[q])
        copy.start()
        copies.append(copy)
    for l in range(slots):
        if l % few == 0:
            copies[l // few].wait()
        tile = fac[l]
        rows = slice(l * n, (l + 1) * n)
        f_pair[rows, :n], f_pair[rows, n:] = halves(tile)
        f_turn[rows, :n], f_turn[rows, n:] = halves(tile.T)


def split_factors(pair_region, factors, per_home):
    _, slots, n, _ = factors.shape
    shape = jax.ShapeDtypeStruct((slots * n, 2 * n), BF16)
    spec = pl.BlockSpec(shape.shape, lambda i, *_: (0, 0))
    return pl.pallas_call(
        functools.partial(split_body, per_home=per_home),
        out_shape=[shape, shape],
        grid_spec=pltpu.PrefetchScalarGridSpec(
            num_scalar_prefetch=1,
            grid=(1,),
            in_specs=[pl.BlockSpec(memory_space=pltpu.HBM)],
            out_specs=[spec, spec],
            scratch_shapes=[pltpu.VMEM((slots, n, n), F32), pltpu.SemaphoreType.DMA((4,))],
        ),
        compiler_params=pltpu.CompilerParams(vmem_limit_bytes=16 << 20),
        cost_estimate=pl.CostEstimate(flops=1 << 20, bytes_accessed=3 << 20, transcendentals=0),
        name="split_factors",
    )(pair_region, pltpu.with_memory_space_constraint(factors, pltpu.HBM))


def deal_body(source, pair_region, owner_map, *refs):
    *outs, regions, owners, sems, small = refs
    count = len(outs)
    copies = []
    for d, out in enumerate(outs):
        to = lax.rem(lax.axis_index("virt") + d, count)
        for i in range(out.shape[0]):
            copies.append(pltpu.make_async_copy(source.at[i, to], out.at[i], sems.at[d, i]))
    copies.append(pltpu.make_async_copy(pair_region, regions, small.at[0]))
    copies.append(pltpu.make_async_copy(owner_map, owners, small.at[1]))
    for copy in copies:
        copy.start()
    for copy in copies:
        copy.wait()


def deal(amplitudes, pair_region, owner_map):
    local, count, n, _ = amplitudes.shape
    anywhere = pl.BlockSpec(memory_space=pl.ANY)
    *pieces, regions, owners = pl.pallas_call(
        deal_body,
        out_shape=[jax.ShapeDtypeStruct((local, n, n), F32)] * count
        + [jax.ShapeDtypeStruct(x.shape, x.dtype) for x in (pair_region, owner_map)],
        in_specs=[anywhere] * 3,
        out_specs=[anywhere] * (count + 2),
        scratch_shapes=[pltpu.SemaphoreType.DMA((count, local)), pltpu.SemaphoreType.DMA((2,))],
        compiler_params=pltpu.CompilerParams(vmem_limit_bytes=4 << 20),
        cost_estimate=pl.CostEstimate(flops=0, bytes_accessed=2 << 20, transcendentals=0),
        name="deal",
    )(*(pltpu.with_memory_space_constraint(x, pltpu.HBM) for x in (amplitudes, pair_region, owner_map)))
    return pieces, regions, owners


def ladder_body(
    codes, touched, *refs, steps
):
    f_pair, f_turn, out, amp_high, amp_low, prod_a, prod_b, grouped = refs[-8:]
    amps = refs[:-8]
    slots, n, _ = out.shape
    entries = codes.shape[1]
    mirrored = (lax.axis_index("pair") >= lax.axis_size("pair") // 2).astype(jnp.int32)

    def put(v, i, tile):
        high, low = halves(tile)
        amp_high[v, :n, i * n : (i + 1) * n] = high
        amp_high[v, n:, i * n : (i + 1) * n] = high
        amp_low[v, :, i * n : (i + 1) * n] = low

    count = len(amps)
    origins = [lax.rem(lax.axis_index("virt") + (count - d), count) for d in steps]

    @pl.when(mirrored == 0)
    def _():
        for v, amp in zip(origins, amps):
            for i in range(amp.shape[0]):
                put(v, i, amp[i])

    @pl.when(mirrored != 0)
    def _():
        for v, amp in zip(origins, amps):
            for i in range(amp.shape[0]):
                put(v, i, amp[i].T)

    chunks = 4
    height = slots * n // chunks
    per = 2 * entries // chunks

    def product(v, prod, q):
        rows = slice(q * height, (q + 1) * height)
        prod[rows] = jnp.dot(
            f_pair[rows], amp_high[v], preferred_element_type=F32
        ) + jnp.dot(f_pair[rows, :n], amp_low[v], preferred_element_type=F32)

    def collect(v, prod, q):
        for e in range(q * per, (q + 1) * per):
            i, k = e // entries, e % entries
            code = codes[2 * v + i, k]
            to = pl.ds(pl.multiple_of(((code >> 8) & 15) * n, n), n)
            source = pl.ds(pl.multiple_of(((code >> 4) & 15) * n, n), n)
            new = prod[source, i * n : (i + 1) * n]
            r = code & 15
            grouped[r, to, :] = jnp.where(code >= FIRST, new, grouped[r, to, :] + new)

    for q in range(chunks):
        product(0, prod_a, q)

    def two(w, c):
        v = 2 * w
        for q in range(chunks):
            product(v + 1, prod_b, q)
            collect(v, prod_a, q)
        for q in range(chunks):
            product(v + 2, prod_a, q)
            collect(v + 1, prod_b, q)
        return c

    lax.fori_loop(0, slots // 4 - 1, two, 0)
    last = slots // 2 - 1
    for q in range(chunks):
        product(last, prod_b, q)
        collect(last - 1, prod_a, q)
    for q in range(chunks):
        collect(last, prod_b, q)

    step = 4
    for g in range(0, slots, step):

        def block(r):
            return jnp.concatenate(
                [
                    jnp.where(touched[o, r] > 0, grouped[r, o * n : (o + 1) * n, :], 0.0)
                    for o in range(g, g + step)
                ],
                axis=0,
            )

        parts = [halves(block(r)) for r in range(slots)]
        high = jnp.concatenate([a for a, _ in parts], axis=1)
        low = jnp.concatenate([b for _, b in parts], axis=1)
        both = jnp.dot(high, f_turn[...], preferred_element_type=F32)
        rest = jnp.dot(low, f_turn[:, :n], preferred_element_type=F32)
        total = both[:, :n] + both[:, n:] + rest
        out[g : g + step] = total.reshape(step, n, n)


def ladder(codes, touched, amps, steps, f_pair, f_turn):
    local, n, _ = amps[0].shape
    slots = local * len(amps)
    wide = slots * n
    few = pl.BlockSpec((local, n, n), lambda i, *_: (0, 0, 0))
    whole = pl.BlockSpec((slots, n, n), lambda i, *_: (0, 0, 0))
    table = pl.BlockSpec((wide, 2 * n), lambda i, *_: (0, 0))
    return pl.pallas_call(
        functools.partial(ladder_body, steps=steps),
        out_shape=jax.ShapeDtypeStruct((slots, n, n), F32),
        grid_spec=pltpu.PrefetchScalarGridSpec(
            num_scalar_prefetch=2,
            grid=(1,),
            in_specs=[few] * len(amps) + [table, table],
            out_specs=whole,
            scratch_shapes=[
                pltpu.VMEM((slots // 2, 2 * n, 2 * n), BF16),
                pltpu.VMEM((slots // 2, n, 2 * n), BF16),
                pltpu.VMEM((wide, 2 * n), F32),
                pltpu.VMEM((wide, 2 * n), F32),
                pltpu.VMEM((slots, wide, n), F32),
            ],
        ),
        compiler_params=pltpu.CompilerParams(vmem_limit_bytes=48 << 20),
        cost_estimate=pl.CostEstimate(
            flops=12 * wide * wide * n, bytes_accessed=4 << 20, transcendentals=0
        ),
        name="ladder",
    )(codes, touched, *amps, f_pair, f_turn)


def pairs_body(spot, blocks, out, *, per_home):
    count = blocks.shape[0]
    homes = count // per_home
    half = count // 2
    out[...] = jnp.zeros(out.shape, F32)

    def home(h, c):
        for v in range(per_home):
            row = v * homes + h
            q = h * per_home + v
            value = blocks[row] + blocks[row + homes // 2]
            out[spot[q]] = value
            out[spot[q + half]] = value
        return c

    lax.fori_loop(0, homes // 2, home, 0)


def join_pairs(spot, blocks, own_slots, per_home):
    def body(spot, blocks, out):
        pairs_body(spot, blocks, out, per_home=per_home)

    return pl.pallas_call(
        body,
        out_shape=jax.ShapeDtypeStruct((own_slots,) + blocks.shape[1:], F32),
        grid_spec=pltpu.PrefetchScalarGridSpec(
            num_scalar_prefetch=1,
            grid=(1,),
            in_specs=[pl.BlockSpec(blocks.shape, lambda i, *_: (0, 0, 0))],
            out_specs=pl.BlockSpec((own_slots,) + blocks.shape[1:], lambda i, *_: (0, 0, 0)),
        ),
        compiler_params=pltpu.CompilerParams(vmem_limit_bytes=16 << 20),
        cost_estimate=pl.CostEstimate(flops=1 << 18, bytes_accessed=3 << 20, transcendentals=0),
        name="join_pairs",
    )(spot, blocks)


def settle(held, blocks, own_most, local_slots, n, group):
    parts = blocks.shape[0]
    per = parts // local_slots

    def body(held, src, out):
        plain = held[0]
        swap = (lax.axis_index("virt") * local_slots < OFF_DIAG).astype(jnp.int32)
        first = pl.program_id(0) * group

        def as_is(g):
            for i in range(local_slots):
                out[i, g] = src[i * per : (i + 1) * per, g].reshape(n, n)

        def turned(g):
            for i in range(local_slots):
                base = jnp.where(swap != 0, local_slots - 1 - i, i) * per
                out[i, g] = src[pl.ds(base, per), g].reshape(n, n).T

        @pl.when(first + group <= plain)
        def _():
            for g in range(group):
                as_is(g)

        @pl.when(first >= plain)
        def _():
            for g in range(group):
                turned(g)

        @pl.when((first < plain) & (first + group > plain))
        def _():
            for g in range(group):
                pl.when(first + g < plain)(functools.partial(as_is, g))
                pl.when(first + g >= plain)(functools.partial(turned, g))

    return pl.pallas_call(
        body,
        out_shape=jax.ShapeDtypeStruct((local_slots, own_most, n, n), F32),
        grid_spec=pltpu.PrefetchScalarGridSpec(
            num_scalar_prefetch=1,
            grid=(own_most // group,),
            in_specs=[
                pl.BlockSpec(
                    (parts, group) + blocks.shape[2:], lambda i, *_: (0, i, 0, 0)
                )
            ],
            out_specs=pl.BlockSpec((local_slots, group, n, n), lambda i, *_: (0, i, 0, 0)),
        ),
        compiler_params=pltpu.CompilerParams(vmem_limit_bytes=16 << 20),
        cost_estimate=pl.CostEstimate(flops=1 << 18, bytes_accessed=4 << 20, transcendentals=0),
        name="settle",
    )(held, blocks)


def on_device(amplitudes, factors, integral_quadruple_table, pair_region, owner_map):
    pair_count = lax.axis_size("pair")
    virt_count = lax.axis_size("virt")
    my_pair = lax.axis_index("pair")
    my_virt = lax.axis_index("virt")
    local_slots, per_home, n, _ = amplitudes.shape
    pair_total = owner_map.shape[0]
    half = pair_total // 2
    own_most = 2 * per_home

    pieces, pair_region, owner_map = deal(amplitudes, pair_region, owner_map)
    amps = {0: pieces[0]}
    for d in sorted(range(1, virt_count), key=lambda d: -min(d, virt_count - d)):
        route = [(i, (i + d) % virt_count) for i in range(virt_count)]
        amps[d] = lax.ppermute(pieces[d], "virt", route)
    near = (1, virt_count - 1)
    pair_region, owner_map, *first = lax.optimization_barrier(
        (pair_region, owner_map, *(amps[d] for d in near))
    )
    amps.update(zip(near, first))
    steps = (0, *near, *sorted(set(range(1, virt_count)) - set(near), key=lambda d: -min(d, virt_count - d)))
    amps = [amps[d] for d in steps]

    pair = my_pair * per_home + my_virt
    mirrored = (pair >= half).astype(jnp.int32)
    mine = jnp.arange(half) == lax.rem(pair, half)
    region = jnp.sum(jnp.where(mine, pair_region, 0))
    here = jnp.arange(integral_quadruple_table.shape[0]) == region
    rows = jnp.sum(jnp.where(here[:, None, None, None], integral_quadruple_table, 0), axis=0)
    o, left, right = rows[..., 0], rows[..., 1], rows[..., 2]
    partner = jnp.where(o < OFF_DIAG, o ^ 1, o)
    codes = jnp.where(
        mirrored != 0, partner * 256 + right * 16 + left, o * 256 + left * 16 + right
    )
    group = ((codes >> 8) * 16 + (codes & 15)).reshape(-1)
    place = jnp.arange(group.shape[0])
    met = (group[:, None] == group[None, :]) & (place[None, :] < place[:, None])
    codes = codes + jnp.where(jnp.any(met, axis=1), 0, FIRST).reshape(codes.shape)
    slot_total = codes.shape[0]
    touched = jnp.any(group[None, :] == jnp.arange(slot_total * 16)[:, None], axis=1)
    touched = touched.astype(jnp.int32).reshape(slot_total, 16)

    same = (owner_map[:, None] == owner_map[None, :]) & (
        jnp.arange(pair_total)[None, :] < jnp.arange(pair_total)[:, None]
    )
    spot = owner_map * own_most + jnp.sum(same.astype(jnp.int32), axis=1)

    plain = jnp.sum((owner_map[:half] == my_pair).astype(jnp.int32))
    held = plain.reshape(1)

    f_pair, f_turn = split_factors(pair_region, factors, per_home)
    amps, codes, touched, f_pair, f_turn, spot, held = lax.optimization_barrier(
        (amps, codes, touched, f_pair, f_turn, spot, held)
    )
    result = ladder(codes, touched, amps, steps, f_pair, f_turn)
    sheets = result.reshape(virt_count * pair_count, -1, n)
    spread = lax.all_to_all(sheets, ("virt", "pair"), split_axis=0, concat_axis=0, tiled=True)
    joined = join_pairs(spot, spread, pair_count * own_most, per_home)
    arrived = lax.all_to_all(joined, "pair", split_axis=0, concat_axis=0, tiled=True)
    return settle(
        held,
        arrived.reshape(pair_count, own_most, -1, n),
        own_most,
        local_slots,
        n,
        8,
    )


def solution(mesh):
    return jax.shard_map(
        on_device,
        mesh=mesh,
        in_specs=(P("virt", "pair", None, None), P(), P(), P(), P()),
        out_specs=P("virt", "pair", None, None),
        check_vma=False,
    )
```
